32 devices in a mesh: seq: 8 (over z, y), batch: 4 (over x, core).
Axes of the slice: x: 2, y: 2, z: 4, core: 2. Of those that a mesh axis runs over, the one named last changes fastest.
Arguments:
- queries: bfloat16 [16384, 384], P(('batch', 'seq')), parts along dimension 0, may hold values from -400 to 400
- key_states: bfloat16 [16384, 384], P(('batch', 'seq')), parts along dimension 0, may hold values from -6 to 6
- value_states: bfloat16 [16384, 384], P(('batch', 'seq')), parts along dimension 0, may hold values from -6 to 6
- grad_output: bfloat16 [16384, 384], P(('batch', 'seq')), parts along dimension 0, may hold values from -6 to 6
- partners: int32 [12, 8], P('batch'), parts along dimension 0, may hold values from 0 to 7, each once within a row
- global_blocks: int32 [8], P('batch'), parts along dimension 0, may hold values from 0 to 7
Outputs:
- attended: bfloat16 [16384, 384], P(('batch', 'seq')), parts along dimension 0
- grad_queries: bfloat16 [16384, 384], P(('batch', 'seq')), parts along dimension 0
- grad_keys: bfloat16 [16384, 384], P(('batch', 'seq')), parts along dimension 0
- grad_values: bfloat16 [16384, 384], P(('batch', 'seq')), parts along dimension 0
The draws below stay inside these ranges and needn't reach their ends.
There are 4 independent parts, one for each index of `batch`. The reference program is written for one: setup_inputs(seed, part) draws one part's arguments, and reference() takes and returns one part's arrays. A program takes and returns all parts, laid end to end along the dimension named above; each array names one. Nothing has to cross between parts.
Inputs may be any that keep to these rules, and one draw needn't show every extreme that they name: `partners`: each row names every sequence block once.
All inputs are finite; a program needn't handle non-finite values.
Results may differ from the reference program's by a relative error of at most 0.0065.
Values may be sent and summed in bfloat16 or wider, within the bound.
No kernel may reach another device: no remote copies, remote signals or barrier semaphores. Data moves between devices by JAX's collectives and lax.ppermute only.
A program may use at most 128 MiB of HBM per device.

```python
import math
import jax
import jax.numpy as jnp
from jax import lax

BLOCK = 512
HEADS = 6
HD = 64
WIDTH = 384
NB = 8
NT = 4096


def joint_draw(key):
    key_field = jnp.clip(jax.random.normal(jax.random.fold_in(key, 11), (NT, HEADS * HD), jnp.float32), -6.0, 6.0)
    query_field = jnp.clip(2.0 * jax.random.normal(jax.random.fold_in(key, 12), (NT, HEADS * HD), jnp.float32), -12.0, 12.0)
    return (query_field, key_field)


def draw_queries(key, part):
    return joint_draw(key)[0].astype(jnp.bfloat16)


def draw_key_states(key, part):
    return joint_draw(key)[1].astype(jnp.bfloat16)


def shard_levels(own_key, shape, shards, smallest, high):
    level = 1.0
    for axis_at, shards_of in shards:
        draws = jax.random.uniform(jax.random.fold_in(jax.random.fold_in(own_key, 6), axis_at), (shards_of,), jnp.float32, smallest / len(shards), high / len(shards))
        level = level * jnp.repeat(jnp.exp(draws), shape[axis_at] // shards_of).reshape((-1,) + (1,) * (len(shape) - 1 - axis_at))
    return level


def noise(stream_key, extent, deviation, reach, pieces=(), kind=jnp.bfloat16):
    entries = jax.random.normal(stream_key, extent, jnp.float32) * deviation
    if len(pieces) > 0:
        entries = shard_levels(stream_key, extent, pieces, -0.22, 0.18) * entries
    return jnp.clip(entries, min=-reach, max=reach).astype(kind)


def setup_inputs(seed: int = 0, part: int = 0) -> dict:
    key_list = jax.random.split(jax.random.key(seed), 7)
    part_keys = jax.random.split(jax.random.fold_in(key_list[6], part), 7)
    return {
        "queries": draw_queries(jax.random.fold_in(jax.random.fold_in(key_list[6], part), 71), part),
        "key_states": draw_key_states(jax.random.fold_in(jax.random.fold_in(key_list[6], part), 71), part),
        "value_states": noise(part_keys[2], (NT, WIDTH), 1.0, 6.0, ((0, 8),)),
        "grad_output": noise(part_keys[3], (NT, WIDTH), 1.0, 6.0, ((0, 8),)),
        "partners": jax.vmap(lambda own: jax.random.permutation(own, NB))(jax.random.split(part_keys[4], 3)).reshape((3, NB)).astype(jnp.int32),
        "global_blocks": jax.random.randint(part_keys[5], (2,), 0, NB).astype(jnp.int32),
    }


def attend_block(query_rows, key_rows, grad_rows):
    length = key_rows.shape[0]
    scale = 1.0 / math.sqrt(HD)
    highest = lax.Precision.HIGHEST
    query_heads = query_rows.astype(jnp.float32).reshape(BLOCK, HEADS, HD)
    key_heads = key_rows[:, :WIDTH].astype(jnp.float32).reshape(length, HEADS, HD)
    value_heads = key_rows[:, WIDTH:].astype(jnp.float32).reshape(length, HEADS, HD)
    grad_heads = grad_rows.astype(jnp.float32).reshape(BLOCK, HEADS, HD)
    scores = jnp.einsum('qhd,khd->hqk', query_heads, key_heads, precision=highest) * scale
    row_peak = lax.optimization_barrier(jnp.max(scores, axis=-1, keepdims=True))
    exponent = jnp.exp(scores - row_peak)
    weights = exponent / lax.optimization_barrier(jnp.sum(exponent, axis=-1, keepdims=True))
    weights_low = weights.astype(jnp.bfloat16).astype(jnp.float32)
    attended = jnp.einsum('hqk,khd->qhd', weights_low, value_heads, precision=highest)
    attended = attended.reshape(BLOCK, WIDTH).astype(jnp.bfloat16)
    grad_weights = jnp.einsum('qhd,khd->hqk', grad_heads, value_heads, precision=highest)
    row_dots = lax.optimization_barrier(jnp.sum(weights * grad_weights, axis=-1, keepdims=True))
    grad_scores = (weights * (grad_weights - row_dots) * scale).astype(jnp.bfloat16).astype(jnp.float32)
    grad_query = jnp.einsum('hqk,khd->qhd', grad_scores, key_heads, precision=highest)
    grad_query = grad_query.reshape(BLOCK, WIDTH).astype(jnp.bfloat16)
    grad_key = jnp.einsum('hqk,qhd->khd', grad_scores, query_heads, precision=highest).reshape(length, WIDTH)
    grad_value = jnp.einsum('hqk,qhd->khd', weights_low, grad_heads, precision=highest).reshape(length, WIDTH)
    return (attended, grad_query, jnp.concatenate([grad_key, grad_value], axis=1))

def reference(queries, key_states, value_states, grad_output, partners, global_blocks):
    key_value = jnp.concatenate([key_states, value_states], axis=1)
    block_ids = jnp.arange(NB, dtype=jnp.int32)
    route_table = jnp.stack([block_ids, (block_ids - 1) % NB, (block_ids + 1) % NB, partners[0], partners[1], partners[2], jnp.full((NB,), global_blocks[0], jnp.int32), jnp.full((NB,), global_blocks[1], jnp.int32)], axis=1).astype(jnp.int32)

    def visit(grad_total, block_index):
        members = route_table[block_index]
        key_rows = jnp.concatenate([lax.dynamic_slice_in_dim(key_value, (members[position] * BLOCK).astype(jnp.int32), BLOCK, 0) for position in range(8)], axis=0)
        start_row = (block_index * BLOCK).astype(jnp.int32)
        query_rows = lax.dynamic_slice_in_dim(queries, start_row, BLOCK, 0)
        grad_rows = lax.dynamic_slice_in_dim(grad_output, start_row, BLOCK, 0)
        attended, grad_query, grad_pair = attend_block(query_rows, key_rows, grad_rows)
        for position in range(8):
            begin_row = (members[position] * BLOCK).astype(jnp.int32)
            current = lax.dynamic_slice_in_dim(grad_total, begin_row, BLOCK, 0)
            grad_total = lax.dynamic_update_slice_in_dim(grad_total, current + grad_pair[position * BLOCK:(position + 1) * BLOCK], begin_row, 0)
        return (grad_total, (attended, grad_query))
    grad_total, (attended, grad_query) = lax.scan(visit, jnp.zeros((NT, 2 * WIDTH), jnp.float32), block_ids)
    return (attended.reshape(NT, WIDTH), grad_query.reshape(NT, WIDTH), grad_total[:, :WIDTH].astype(jnp.bfloat16), grad_total[:, WIDTH:].astype(jnp.bfloat16))
```

```python
import math

import jax
import jax.numpy as jnp
from jax import lax
from jax.experimental import pallas as pl
from jax.experimental.pallas import tpu as pltpu
from jax.sharding import PartitionSpec as P

HEADS = 6
HD = 64


def extended(x, sides, width):
    for axis, dim in sides:
        devices, length = (lax.axis_size(axis), x.shape[dim])
        up = [(i, (i + 1) % devices) for i in range(devices)]
        down = [(j, i) for i, j in up]
        last = lax.slice_in_dim(x, length - width, length, axis=dim)
        first = lax.slice_in_dim(x, 0, width, axis=dim)
        before = lax.ppermute(last, axis, up)
        after = lax.ppermute(first, axis, down)
        x = jnp.concatenate([before, x, after], axis=dim)
    return x


def from_behind(x, axis, by):
    devices = lax.axis_size(axis)
    return lax.ppermute(x, axis, [(i, (i + by) % devices) for i in range(devices)])


def head_split(matrix):
    return matrix.reshape(matrix.shape[0], HEADS, HD).transpose(1, 0, 2)


def head_join(stacked):
    return stacked.transpose(1, 0, 2).reshape(stacked.shape[1], HEADS * HD)


def attend(queries, key_rows, grad_output):
    features = queries.shape[1]
    scale = 1.0 / math.sqrt(HD)
    contract_last = (((1,), (1,)), ((), ()))
    contract_first = (((0,), (0,)), ((), ()))

    def per_head(head_items):
        query_head, key_head, value_head, grad_head = head_items
        scores = (
            lax.dot_general(query_head, key_head, contract_last, preferred_element_type=jnp.float32)
            * scale
        )
        row_peak = jnp.max(scores, axis=-1, keepdims=True)
        exponent = jnp.exp(scores - row_peak)
        weights = exponent / jnp.sum(exponent, axis=-1, keepdims=True)
        weights_low = weights.astype(jnp.bfloat16)
        output_head = jnp.dot(weights_low, value_head, preferred_element_type=jnp.float32).astype(
            jnp.bfloat16
        )
        grad_weights = lax.dot_general(
            grad_head, value_head, contract_last, preferred_element_type=jnp.float32
        )
        row_dots = jnp.sum(weights * grad_weights, axis=-1, keepdims=True)
        grad_scores = (weights * (grad_weights - row_dots) * scale).astype(jnp.bfloat16)
        grad_query = jnp.dot(grad_scores, key_head, preferred_element_type=jnp.float32).astype(
            jnp.bfloat16
        )
        grad_key = lax.dot_general(
            grad_scores, query_head, contract_first, preferred_element_type=jnp.float32
        )
        grad_value = lax.dot_general(
            weights_low, grad_head, contract_first, preferred_element_type=jnp.float32
        )
        return (output_head, grad_query, grad_key, grad_value)

    outputs, grad_query, grad_key, grad_value = lax.map(
        per_head,
        (
            head_split(queries),
            head_split(key_rows[:, :features]),
            head_split(key_rows[:, features:]),
            head_split(grad_output),
        ),
    )
    grad_pair = jnp.concatenate([head_join(grad_key), head_join(grad_value)], axis=1)
    return (head_join(outputs), head_join(grad_query), grad_pair)


def route_forward(key_value, route_table, devices):
    block_rows, columns = key_value.shape
    pieces = key_value.reshape(devices, block_rows // devices, columns)
    spread = lax.all_to_all(pieces, "seq", split_axis=0, concat_axis=0, tiled=True)
    picked = jnp.take(spread, route_table, axis=0)
    arrived = lax.all_to_all(picked, "seq", split_axis=1, concat_axis=1, tiled=True)
    return arrived.reshape(route_table.shape[0], block_rows, columns)


def route_back(grad_terms, route_table, devices):
    routes, block_rows, columns = grad_terms.shape
    piece_rows = block_rows // devices
    pieces = grad_terms.reshape(routes, devices, piece_rows, columns)
    coming = lax.all_to_all(pieces, "seq", split_axis=1, concat_axis=1, tiled=True)
    block_ids = jnp.arange(devices, dtype=jnp.int32)
    one_hot = (route_table[:, :, None] == block_ids[None, None, :]).astype(jnp.float32)
    summed = jnp.einsum(
        "rds,rdx->sx",
        one_hot,
        coming.reshape(routes, devices, piece_rows * columns),
        precision=lax.Precision.HIGHEST,
    )
    returned = lax.all_to_all(
        summed.reshape(devices, piece_rows, columns), "seq", split_axis=0, concat_axis=0, tiled=True
    )
    return returned.reshape(block_rows, columns)


def routed_local(queries, key_states, value_states, grad_output, partners, global_blocks):
    devices = lax.axis_size("seq")
    block_rows = queries.shape[0]
    features = queries.shape[1]
    key_value = jnp.concatenate([key_states, value_states], axis=1)
    table_rows = []
    table_rows = table_rows + [partners[0], partners[1], partners[2]]
    table_rows = table_rows + [
        jnp.full((devices,), global_blocks[0], jnp.int32),
        jnp.full((devices,), global_blocks[1], jnp.int32),
    ]
    route_table = jnp.stack(table_rows)
    fetched = route_forward(key_value, route_table, devices)
    padded = extended(key_value, (("seq", 0),), block_rows)
    left_block = padded[:block_rows]
    right_block = padded[2 * block_rows :]
    offset = 0
    random_blocks = [fetched[offset], fetched[offset + 1], fetched[offset + 2]]
    global_rows = [fetched[offset + 3], fetched[offset + 4]]
    key_rows = jnp.concatenate(
        [key_value, left_block, right_block] + random_blocks + global_rows, axis=0
    )
    attended, grad_queries, grad_pair = attend(queries, key_rows, grad_output)
    grad_parts = grad_pair.reshape(8, block_rows, 2 * features)
    grad_total = grad_parts[0]
    returning = []
    grad_total = grad_total + from_behind(grad_parts[1], "seq", -1)
    grad_total = grad_total + from_behind(grad_parts[2], "seq", 1)
    returning = returning + [grad_parts[3], grad_parts[4], grad_parts[5]]
    returning = returning + [grad_parts[6], grad_parts[7]]
    grad_total = grad_total + route_back(jnp.stack(returning), route_table, devices)
    return (
        attended,
        grad_queries,
        grad_total[:, :features].astype(jnp.bfloat16),
        grad_total[:, features:].astype(jnp.bfloat16),
    )


LISTED = 8
TO_LOG2 = 1.0 / (math.log(2.0) * math.sqrt(HD))
VMEM_LIMIT = 56 * 1024 * 1024


def matmul(a, b, contract_a, contract_b):
    return lax.dot_general(
        a, b, (((contract_a,), (contract_b,)), ((), ())), preferred_element_type=jnp.float32
    )


def placed(rows, side):
    blank = jnp.zeros_like(rows)
    return jnp.concatenate([rows, blank] if side == 0 else [blank, rows], axis=0)


def pair_kernel(first, bias_ref, q_ref, do_ref, k_ref, v_ref, *refs):
    if first:
        e_ref, u_ref, acc_out, run_out, pair_out = refs
    else:
        acc_in, run_in, e_ref, u_ref, acc_out, run_out, pair_out = refs
    keys = k_ref[...]
    values = v_ref[...]
    q_t = q_ref[...].T
    do_t = do_ref[...].T
    k_t = keys.T
    v_t = values.T
    bias = bias_ref[0]
    for side in range(2):
        rows = slice(side * HD, (side + 1) * HD)
        scores = matmul(keys, placed(q_t[rows], side), 1, 0) * TO_LOG2
        peak = jnp.max(scores, axis=0, keepdims=True)
        exponent = jnp.exp2(scores - peak)
        total = jnp.sum(exponent, axis=0, keepdims=True)
        low = exponent.astype(jnp.bfloat16)
        e_ref[side] = low
        both = matmul(jnp.concatenate([v_t[rows], k_t[rows]], axis=0), low, 1, 0)
        grad_weights = matmul(values, placed(do_t[rows], side), 1, 0)
        dots = jnp.sum(both[:HD] * do_t[rows].astype(jnp.float32), axis=0, keepdims=True)
        mean = dots / total
        centred = (exponent * (grad_weights - mean)).astype(jnp.bfloat16)
        u_ref[side] = centred
        moved = matmul(k_t[rows], centred, 1, 0) + mean * both[HD:]
        peak = peak + bias
        if first:
            acc_out[side, : 2 * HD] = both
            acc_out[side, 2 * HD :] = moved
            top, run_total, run_dots = peak, total, dots
        else:
            old = run_in[side, 0:1]
            top = jnp.maximum(old, peak)
            keep = jnp.exp2(old - top)
            take = jnp.exp2(peak - top)
            acc_out[side, : 2 * HD] = acc_in[side, : 2 * HD] * keep + both * take
            acc_out[side, 2 * HD :] = acc_in[side, 2 * HD :] * keep + moved * take
            run_total = run_in[side, 1:2] * keep + total * take
            run_dots = run_in[side, 2:3] * keep + dots * take
        run_out[side, 0:1] = top
        run_out[side, 1:2] = run_total
        run_out[side, 2:3] = run_dots
        pair_out[side, 0:1] = peak
        pair_out[side, 1:2] = mean


def head_pairs(features):
    return features // (2 * HD)


def column_spec(rows, offset):
    return pl.BlockSpec((rows, 2 * HD), lambda p: (0, p + offset))


def per_head_spec(*tail):
    return pl.BlockSpec((2,) + tail, lambda p: (p,) + (0,) * len(tail))


def pair_terms(bias, query_grad, key_value, running):
    rows, columns = query_grad.shape
    keys = key_value.shape[0]
    features = columns // 2
    steps = head_pairs(features)
    heads = 2 * steps
    first = running is None
    state = [] if first else list(running)
    acc = jax.ShapeDtypeStruct((heads, 3 * HD, rows), jnp.float32)
    stat = jax.ShapeDtypeStruct((heads, 8, rows), jnp.float32)
    big = jax.ShapeDtypeStruct((heads, keys, rows), jnp.bfloat16)
    acc_spec = per_head_spec(3 * HD, rows)
    stat_spec = per_head_spec(8, rows)
    big_spec = per_head_spec(keys, rows)
    return pl.pallas_call(
        lambda *refs: pair_kernel(first, *refs),
        grid=(steps,),
        in_specs=[
            pl.BlockSpec(memory_space=pltpu.SMEM),
            column_spec(rows, 0),
            column_spec(rows, steps),
            column_spec(keys, 0),
            column_spec(keys, steps),
        ]
        + ([] if first else [acc_spec, stat_spec]),
        out_specs=[big_spec, big_spec, acc_spec, stat_spec, stat_spec],
        out_shape=[big, big, acc, stat, stat],
        name="pair_first" if first else "pair_next",
        compiler_params=pltpu.CompilerParams(vmem_limit_bytes=VMEM_LIMIT),
        cost_estimate=pl.CostEstimate(
            flops=8 * heads * HD * rows * keys,
            transcendentals=heads * rows * keys,
            bytes_accessed=4 * heads * rows * keys,
        ),
    )(bias, query_grad, query_grad, key_value, key_value, *state)


def joined(mine, other, side):
    top = jnp.maximum(mine[side, 0:1], other[side, 0:1])
    here = jnp.exp2(mine[side, 0:1] - top)
    there = jnp.exp2(other[side, 0:1] - top)
    inverse = 1.0 / (mine[side, 1:2] * here + other[side, 1:2] * there)
    mean = (mine[side, 2:3] * here + other[side, 2:3] * there) * inverse
    return top, inverse, mean


def key_kernel(*refs):
    out_k, out_v = refs[-2:]
    scale = 1.0 / math.sqrt(HD)
    k_total = None
    v_total = None
    for at in range(0, len(refs) - 2, 7):
        e_ref, u_ref, q_ref, do_ref, pair_ref, mine, other = refs[at : at + 7]
        q_t = q_ref[...].T.astype(jnp.float32)
        do_t = do_ref[...].T.astype(jnp.float32)
        for side in range(2):
            rows = slice(side * HD, (side + 1) * HD)
            top, inverse, mean = joined(mine, other, side)
            factor = jnp.exp2(pair_ref[side, 0:1] - top) * inverse
            shift = pair_ref[side, 1:2] - mean
            scaled_q = q_t[rows] * (factor * scale)
            for_e = jnp.concatenate(
                [
                    placed((scaled_q * shift).astype(jnp.bfloat16), side),
                    placed((do_t[rows] * factor).astype(jnp.bfloat16), side),
                ],
                axis=0,
            )
            from_e = matmul(e_ref[side], for_e, 1, 1)
            from_u = matmul(u_ref[side], placed(scaled_q.astype(jnp.bfloat16), side), 1, 1)
            k_part = from_e[:, : 2 * HD] + from_u
            v_part = from_e[:, 2 * HD :]
            k_total = k_part if k_total is None else k_total + k_part
            v_total = v_part if v_total is None else v_total + v_part
    out_k[...] = k_total.astype(out_k.dtype)
    out_v[...] = v_total.astype(out_v.dtype)


def key_terms(entries, dtype):
    heads, keys, rows = entries[0][0].shape
    steps = heads // 2
    operands = []
    in_specs = []
    for e, u, query_grad, pair, mine, other in entries:
        operands += [e, u, query_grad, query_grad, pair, mine, other]
        in_specs += [
            per_head_spec(keys, rows),
            per_head_spec(keys, rows),
            column_spec(rows, 0),
            column_spec(rows, steps),
            per_head_spec(8, rows),
            per_head_spec(8, rows),
            per_head_spec(8, rows),
        ]
    return pl.pallas_call(
        key_kernel,
        grid=(steps,),
        in_specs=in_specs,
        out_specs=[column_spec(keys, 0), column_spec(keys, 0)],
        out_shape=[jax.ShapeDtypeStruct((keys, heads * HD), dtype)] * 2,
        name="key_terms",
        compiler_params=pltpu.CompilerParams(vmem_limit_bytes=VMEM_LIMIT),
        cost_estimate=pl.CostEstimate(
            flops=len(entries) * 6 * heads * HD * rows * keys,
            transcendentals=0,
            bytes_accessed=len(entries) * 4 * heads * rows * keys,
        ),
    )(*operands)


def query_kernel(final, acc, mine, other, *refs):
    if final:
        far_o, far_q, out_o, out_q = refs
    else:
        out_o, out_q = refs
    scale = 1.0 / math.sqrt(HD)
    outs = []
    grads = []
    for side in range(2):
        top, inverse, mean = joined(mine, other, side)
        factor = jnp.exp2(mine[side, 0:1] - top) * inverse
        outs.append(acc[side, :HD] * factor)
        grads.append((acc[side, 2 * HD :] - acc[side, HD : 2 * HD] * mean) * (factor * scale))
    out_rows = jnp.concatenate(outs, axis=0).T
    grad_rows = jnp.concatenate(grads, axis=0).T
    if final:
        out_rows = out_rows + far_o[...].astype(jnp.float32)
        grad_rows = grad_rows + far_q[...].astype(jnp.float32)
    out_o[...] = out_rows.astype(out_o.dtype)
    out_q[...] = grad_rows.astype(out_q.dtype)


def query_terms(acc, mine, other, far):
    heads, _, rows = acc.shape
    steps = heads // 2
    final = far is not None
    extra = list(far) if final else []
    return pl.pallas_call(
        lambda *refs: query_kernel(final, *refs),
        grid=(steps,),
        in_specs=[per_head_spec(3 * HD, rows), per_head_spec(8, rows), per_head_spec(8, rows)]
        + [column_spec(rows, 0)] * len(extra),
        out_specs=[column_spec(rows, 0), column_spec(rows, 0)],
        out_shape=[jax.ShapeDtypeStruct((rows, heads * HD), jnp.bfloat16)] * 2,
        name="query_final" if final else "query_send",
        compiler_params=pltpu.CompilerParams(vmem_limit_bytes=VMEM_LIMIT),
        cost_estimate=pl.CostEstimate(
            flops=8 * heads * HD * rows, transcendentals=0, bytes_accessed=16 * heads * HD * rows
        ),
    )(acc, mine, other, *extra)


def swapped(x, offset):
    devices = lax.axis_size("seq")
    return lax.ppermute(x, "seq", [(i, i ^ offset) for i in range(devices)])


def repeats(partners, global_blocks, query_block, key_block, devices):
    listed = [query_block, (query_block - 1) % devices, (query_block + 1) % devices]
    listed += [lax.dynamic_index_in_dim(partners[r], query_block, 0, False) for r in range(3)]
    listed += [global_blocks[0], global_blocks[1]]
    count = sum((entry == key_block).astype(jnp.float32) for entry in listed)
    return jnp.where(count > 0.0, jnp.log2(jnp.maximum(count, 1.0)), -1e30).reshape(1)


def dense_local(queries, key_states, value_states, grad_output, partners, global_blocks):
    devices = lax.axis_size("seq")
    far = devices // 2
    me = lax.axis_index("seq")
    key_value = jnp.concatenate([key_states, value_states], axis=1)
    query_grad = jnp.concatenate([queries, grad_output], axis=1)
    offsets = list(range(far))
    key_blocks = [key_value] + [swapped(key_value, o) for o in offsets[1:]]
    query_blocks = [query_grad, swapped(query_grad, far)]
    running = [None, None]
    saved = {}
    for at in [(0, k) for k in offsets] + [(1, k) for k in offsets]:
        q, k = at
        bias = repeats(partners, global_blocks, me ^ (q * far), me ^ offsets[k], devices)
        e, u, acc, run, pair = pair_terms(bias, query_blocks[q], key_blocks[k], running[q])
        running[q] = (acc, run)
        saved[at] = (e, u, query_blocks[q], pair)
    theirs = swapped(jnp.stack([running[1][1], running[0][1]]), far)
    others = [theirs[0], theirs[1]]
    sent = query_terms(running[1][0], running[1][1], others[1], None)
    came = [swapped(x, far) for x in sent]
    key_parts = []
    for k in reversed(offsets):
        entries = [saved[(q, k)] + (running[q][1], others[q]) for q in range(2)]
        parts = key_terms(entries, jnp.float32 if k == 0 else jnp.bfloat16)
        key_parts.append(parts if k == 0 else [swapped(x, offsets[k]) for x in parts])
    attended, grad_queries = query_terms(running[0][0], running[0][1], others[0], came)
    grads = [
        sum(parts[i].astype(jnp.float32) for parts in key_parts).astype(jnp.bfloat16)
        for i in range(2)
    ]
    return (attended, grad_queries, grads[0], grads[1])


def local(*operands):
    devices = lax.axis_size("seq")
    paired = devices >= 4 and devices & (devices - 1) == 0
    return (dense_local if paired and devices <= LISTED else routed_local)(*operands)


def solution(mesh):
    in_specs = (
        P(("batch", "seq"), None),
        P(("batch", "seq"), None),
        P(("batch", "seq"), None),
        P(("batch", "seq"), None),
        P("batch", None),
        P("batch"),
    )
    out_specs = (
        P(("batch", "seq"), None),
        P(("batch", "seq"), None),
        P(("batch", "seq"), None),
        P(("batch", "seq"), None),
    )
    return jax.shard_map(local, mesh=mesh, in_specs=in_specs, out_specs=out_specs, check_vma=False)
```

```python
import math

import jax
import jax.numpy as jnp
from jax import lax
from jax.experimental import pallas as pl
from jax.experimental.pallas import tpu as pltpu
from jax.sharding import PartitionSpec as P

HEADS = 6
HD = 64


def extended(x, sides, width):
    for axis, dim in sides:
        devices, length = (lax.axis_size(axis), x.shape[dim])
        up = [(i, (i + 1) % devices) for i in range(devices)]
        down = [(j, i) for i, j in up]
        last = lax.slice_in_dim(x, length - width, length, axis=dim)
        first = lax.slice_in_dim(x, 0, width, axis=dim)
        before = lax.ppermute(last, axis, up)
        after = lax.ppermute(first, axis, down)
        x = jnp.concatenate([before, x, after], axis=dim)
    return x


def from_behind(x, axis, by):
    devices = lax.axis_size(axis)
    return lax.ppermute(x, axis, [(i, (i + by) % devices) for i in range(devices)])


def head_split(matrix):
    return matrix.reshape(matrix.shape[0], HEADS, HD).transpose(1, 0, 2)


def head_join(stacked):
    return stacked.transpose(1, 0, 2).reshape(stacked.shape[1], HEADS * HD)


def attend(queries, key_rows, grad_output):
    features = queries.shape[1]
    scale = 1.0 / math.sqrt(HD)
    contract_last = (((1,), (1,)), ((), ()))
    contract_first = (((0,), (0,)), ((), ()))

    def per_head(head_items):
        query_head, key_head, value_head, grad_head = head_items
        scores = (
            lax.dot_general(query_head, key_head, contract_last, preferred_element_type=jnp.float32)
            * scale
        )
        row_peak = jnp.max(scores, axis=-1, keepdims=True)
        exponent = jnp.exp(scores - row_peak)
        weights = exponent / jnp.sum(exponent, axis=-1, keepdims=True)
        weights_low = weights.astype(jnp.bfloat16)
        output_head = jnp.dot(weights_low, value_head, preferred_element_type=jnp.float32).astype(
            jnp.bfloat16
        )
        grad_weights = lax.dot_general(
            grad_head, value_head, contract_last, preferred_element_type=jnp.float32
        )
        row_dots = jnp.sum(weights * grad_weights, axis=-1, keepdims=True)
        grad_scores = (weights * (grad_weights - row_dots) * scale).astype(jnp.bfloat16)
        grad_query = jnp.dot(grad_scores, key_head, preferred_element_type=jnp.float32).astype(
            jnp.bfloat16
        )
        grad_key = lax.dot_general(
            grad_scores, query_head, contract_first, preferred_element_type=jnp.float32
        )
        grad_value = lax.dot_general(
            weights_low, grad_head, contract_first, preferred_element_type=jnp.float32
        )
        return (output_head, grad_query, grad_key, grad_value)

    outputs, grad_query, grad_key, grad_value = lax.map(
        per_head,
        (
            head_split(queries),
            head_split(key_rows[:, :features]),
            head_split(key_rows[:, features:]),
            head_split(grad_output),
        ),
    )
    grad_pair = jnp.concatenate([head_join(grad_key), head_join(grad_value)], axis=1)
    return (head_join(outputs), head_join(grad_query), grad_pair)


def route_forward(key_value, route_table, devices):
    block_rows, columns = key_value.shape
    pieces = key_value.reshape(devices, block_rows // devices, columns)
    spread = lax.all_to_all(pieces, "seq", split_axis=0, concat_axis=0, tiled=True)
    picked = jnp.take(spread, route_table, axis=0)
    arrived = lax.all_to_all(picked, "seq", split_axis=1, concat_axis=1, tiled=True)
    return arrived.reshape(route_table.shape[0], block_rows, columns)


def route_back(grad_terms, route_table, devices):
    routes, block_rows, columns = grad_terms.shape
    piece_rows = block_rows // devices
    pieces = grad_terms.reshape(routes, devices, piece_rows, columns)
    coming = lax.all_to_all(pieces, "seq", split_axis=1, concat_axis=1, tiled=True)
    block_ids = jnp.arange(devices, dtype=jnp.int32)
    one_hot = (route_table[:, :, None] == block_ids[None, None, :]).astype(jnp.float32)
    summed = jnp.einsum(
        "rds,rdx->sx",
        one_hot,
        coming.reshape(routes, devices, piece_rows * columns),
        precision=lax.Precision.HIGHEST,
    )
    returned = lax.all_to_all(
        summed.reshape(devices, piece_rows, columns), "seq", split_axis=0, concat_axis=0, tiled=True
    )
    return returned.reshape(block_rows, columns)


def routed_local(queries, key_states, value_states, grad_output, partners, global_blocks):
    devices = lax.axis_size("seq")
    block_rows = queries.shape[0]
    features = queries.shape[1]
    key_value = jnp.concatenate([key_states, value_states], axis=1)
    table_rows = []
    table_rows = table_rows + [partners[0], partners[1], partners[2]]
    table_rows = table_rows + [
        jnp.full((devices,), global_blocks[0], jnp.int32),
        jnp.full((devices,), global_blocks[1], jnp.int32),
    ]
    route_table = jnp.stack(table_rows)
    fetched = route_forward(key_value, route_table, devices)
    padded = extended(key_value, (("seq", 0),), block_rows)
    left_block = padded[:block_rows]
    right_block = padded[2 * block_rows :]
    offset = 0
    random_blocks = [fetched[offset], fetched[offset + 1], fetched[offset + 2]]
    global_rows = [fetched[offset + 3], fetched[offset + 4]]
    key_rows = jnp.concatenate(
        [key_value, left_block, right_block] + random_blocks + global_rows, axis=0
    )
    attended, grad_queries, grad_pair = attend(queries, key_rows, grad_output)
    grad_parts = grad_pair.reshape(8, block_rows, 2 * features)
    grad_total = grad_parts[0]
    returning = []
    grad_total = grad_total + from_behind(grad_parts[1], "seq", -1)
    grad_total = grad_total + from_behind(grad_parts[2], "seq", 1)
    returning = returning + [grad_parts[3], grad_parts[4], grad_parts[5]]
    returning = returning + [grad_parts[6], grad_parts[7]]
    grad_total = grad_total + route_back(jnp.stack(returning), route_table, devices)
    return (
        attended,
        grad_queries,
        grad_total[:, :features].astype(jnp.bfloat16),
        grad_total[:, features:].astype(jnp.bfloat16),
    )


LISTED = 8
TO_LOG2 = 1.0 / (math.log(2.0) * math.sqrt(HD))
VMEM_LIMIT = 60 * 1024 * 1024
CHUNK = 256


def matmul(a, b, contract_a, contract_b):
    return lax.dot_general(
        a, b, (((contract_a,), (contract_b,)), ((), ())), preferred_element_type=jnp.float32
    )


def placed(rows, side):
    blank = jnp.zeros_like(rows)
    return jnp.concatenate([rows, blank] if side == 0 else [blank, rows], axis=0)


def listed_times(partners_ref, globals_ref, query_block, key_block, devices):
    count = jnp.int32(0)
    entries = [query_block, lax.rem(query_block + devices - 1, devices)]
    entries += [lax.rem(query_block + 1, devices)]
    entries += [partners_ref[r, query_block] for r in range(partners_ref.shape[0])]
    entries += [globals_ref[g] for g in range(globals_ref.shape[0])]
    for entry in entries:
        count = count + jnp.where(entry == key_block, 1, 0)
    return count


def pair_kernel(first, moves, partners_ref, globals_ref, q_ref, do_ref, k_ref, v_ref, *refs):
    if first:
        e_ref, u_ref, acc_out, run_out, pair_out, e_buf, u_buf, sems = refs
    else:
        acc_in, run_in, e_ref, u_ref, acc_out, run_out, pair_out, e_buf, u_buf, sems = refs
    devices = lax.axis_size("seq")
    me = lax.axis_index("seq")
    count = listed_times(
        partners_ref, globals_ref, me ^ moves[0], me ^ moves[1], devices
    ).astype(jnp.float32)
    bias = jnp.log2(jnp.full((1, CHUNK), jnp.maximum(count, 1.0), jnp.float32))
    bias = jnp.where(count > 0.0, bias, -1e30)
    heads, keys_count, rows_count = e_buf.shape
    ones = jnp.ones((16, keys_count), jnp.bfloat16)
    chunks = rows_count // CHUNK
    units = [(head, at) for head in range(heads) for at in range(chunks)]
    halves = [slice(0, HD), slice(HD, 2 * HD)]
    lanes = [slice(at * CHUNK, (at + 1) * CHUNK) for at in range(chunks)]
    state = [{} for _ in units]
    ready = {}
    copies = []

    def operands(head):
        step = head // 2
        if step not in ready:
            cols = slice(step * 2 * HD, (step + 1) * 2 * HD)
            keys = k_ref[:, cols]
            values = v_ref[:, cols]
            q_t = q_ref[:, cols].T.astype(jnp.float32) * TO_LOG2
            q_high = q_t.astype(jnp.bfloat16)
            q_low = (q_t - q_high.astype(jnp.float32)).astype(jnp.bfloat16)
            ready[step] = dict(
                twice=jnp.concatenate([keys, keys], axis=1),
                values=values,
                q_high=q_high,
                q_low=q_low,
                do_t=do_ref[:, cols].T,
                k_t=keys.T,
                v_t=values.T,
            )
        return ready[step]

    def products(n):
        head, at = units[n]
        side, cols = head % 2, lanes[at]
        rows = halves[side]
        ops = operands(head)
        both_q = [placed(ops[name][rows, cols], side) for name in ("q_high", "q_low")]
        state[n]["scores"] = matmul(ops["twice"], jnp.concatenate(both_q, axis=0), 1, 0)

    def exponents(n):
        head, at = units[n]
        scores = state[n].pop("scores")
        peak = jnp.max(scores, axis=0, keepdims=True)
        low = jnp.exp2(scores - peak).astype(jnp.bfloat16)
        e_buf[head, :, lanes[at]] = low
        state[n]["peak"] = peak
        state[n]["low"] = low

    def sums(n):
        head, at = units[n]
        rows = halves[head % 2]
        ops = operands(head)
        left = jnp.concatenate([ops["v_t"][rows], ops["k_t"][rows], ones], axis=0)
        state[n]["both"] = matmul(left, state[n]["low"], 1, 0)

    def centre(n):
        head, at = units[n]
        side, cols = head % 2, lanes[at]
        ops = operands(head)
        both = state[n]["both"]
        total = both[2 * HD : 2 * HD + 1]
        do_t = ops["do_t"][halves[side], cols]
        dots = jnp.sum(both[:HD] * do_t.astype(jnp.float32), axis=0, keepdims=True)
        mean = dots / total
        grad = matmul(ops["values"], placed(do_t, side), 1, 0)
        centred = state[n].pop("low") * (grad - mean).astype(jnp.bfloat16)
        u_buf[head, :, cols] = centred
        state[n].update(total=total, dots=dots, mean=mean, centred=centred)

    def finish(n):
        head, at = units[n]
        side, cols = head % 2, lanes[at]
        step = head // 2
        one = state[n]
        both = one["both"]
        moved = matmul(operands(head)["k_t"][halves[side]], one["centred"], 1, 0)
        moved = moved + one["mean"] * both[HD : 2 * HD]
        peak = one["peak"] + bias
        if first:
            acc_out[head, : 2 * HD, cols] = both[: 2 * HD]
            acc_out[head, 2 * HD :, cols] = moved
            top, total, dots = peak, one["total"], one["dots"]
        else:
            at_row = 3 * side
            old = run_in[step, at_row : at_row + 1, cols]
            top = jnp.maximum(old, peak)
            keep = jnp.exp2(old - top)
            take = jnp.exp2(peak - top)
            acc_out[head, : 2 * HD, cols] = (
                acc_in[head, : 2 * HD, cols] * keep + both[: 2 * HD] * take
            )
            acc_out[head, 2 * HD :, cols] = acc_in[head, 2 * HD :, cols] * keep + moved * take
            total = run_in[step, at_row + 1 : at_row + 2, cols] * keep + one["total"] * take
            dots = run_in[step, at_row + 2 : at_row + 3, cols] * keep + one["dots"] * take
        for row, value in enumerate((top, total, dots)):
            run_out[step, 3 * side + row : 3 * side + row + 1, cols] = value
        for row, value in enumerate((peak, one["mean"])):
            pair_out[step, 3 * side + row : 3 * side + row + 1, cols] = value
        state[n].clear()
        if at == chunks - 1:
            for which, (source, target) in enumerate(((e_buf, e_ref), (u_buf, u_ref))):
                copy = pltpu.make_async_copy(
                    source.at[head], target.at[head], sems.at[which, head]
                )
                copy.start()
                copies.append(copy)

    for t in range(len(units) + 3):
        if 0 <= t - 3:
            finish(t - 3)
        if 0 <= t - 2 < len(units):
            centre(t - 2)
        if 0 <= t - 1 < len(units):
            exponents(t - 1)
            sums(t - 1)
        if t < len(units):
            products(t)
    for copy in copies:
        copy.wait()


def head_pairs(features):
    return features // (2 * HD)


def column_spec(rows, offset):
    return pl.BlockSpec((rows, 2 * HD), lambda p: (0, p + offset))


def per_head_spec(*tail):
    return pl.BlockSpec((2,) + tail, lambda p: (p,) + (0,) * len(tail))


def stat_rows(rows):
    return pl.BlockSpec((1, 8, rows), lambda p: (p, 0, 0))


def half_spec(rows, features, which):
    return pl.BlockSpec((rows, features), lambda p: (0, which))


def pair_terms(tables, moves, query_grad, key_value, running):
    rows, columns = query_grad.shape
    keys = key_value.shape[0]
    features = columns // 2
    steps = head_pairs(features)
    heads = 2 * steps
    first = running is None
    state = [] if first else list(running)
    acc = jax.ShapeDtypeStruct((heads, 3 * HD, rows), jnp.float32)
    stat = jax.ShapeDtypeStruct((steps, 8, rows), jnp.float32)
    big = jax.ShapeDtypeStruct((heads, keys, rows), jnp.bfloat16)
    whole = pl.BlockSpec(memory_space=pltpu.VMEM)
    far = pl.BlockSpec(memory_space=pl.ANY)
    small = pl.BlockSpec(memory_space=pltpu.SMEM)
    return pl.pallas_call(
        lambda *refs: pair_kernel(first, moves, *refs),
        grid=(1,),
        in_specs=[
            small,
            small,
            half_spec(rows, features, 0),
            half_spec(rows, features, 1),
            half_spec(keys, features, 0),
            half_spec(keys, features, 1),
        ]
        + [whole] * len(state),
        out_specs=[far, far, whole, whole, whole],
        out_shape=[big, big, acc, stat, stat],
        scratch_shapes=[
            pltpu.VMEM(big.shape, big.dtype),
            pltpu.VMEM(big.shape, big.dtype),
            pltpu.SemaphoreType.DMA((2, heads)),
        ],
        name="pair_first" if first else "pair_next",
        compiler_params=pltpu.CompilerParams(vmem_limit_bytes=VMEM_LIMIT),
        cost_estimate=pl.CostEstimate(
            flops=8 * heads * HD * rows * keys,
            transcendentals=heads * rows * keys,
            bytes_accessed=4 * heads * rows * keys,
        ),
    )(*tables, query_grad, query_grad, key_value, key_value, *state)


def joined(mine, other, side):
    at = 3 * side
    top = jnp.maximum(mine[0, at : at + 1], other[0, at : at + 1])
    here = jnp.exp2(mine[0, at : at + 1] - top)
    there = jnp.exp2(other[0, at : at + 1] - top)
    inverse = 1.0 / (mine[0, at + 1 : at + 2] * here + other[0, at + 1 : at + 2] * there)
    mean = (mine[0, at + 2 : at + 3] * here + other[0, at + 2 : at + 3] * there) * inverse
    return top, inverse, mean


def key_kernel(*refs):
    out_k, out_v = refs[-2:]
    scale = 1.0 / math.sqrt(HD)
    k_total = None
    v_total = None
    for at in range(0, len(refs) - 2, 7):
        e_ref, u_ref, q_ref, do_ref, pair_ref, mine, other = refs[at : at + 7]
        q_t = q_ref[...].T.astype(jnp.float32)
        do_t = do_ref[...].T.astype(jnp.float32)
        for side in range(2):
            rows = slice(side * HD, (side + 1) * HD)
            top, inverse, mean = joined(mine, other, side)
            factor = jnp.exp2(pair_ref[0, 3 * side : 3 * side + 1] - top) * inverse
            shift = pair_ref[0, 3 * side + 1 : 3 * side + 2] - mean
            scaled_q = q_t[rows] * (factor * scale)
            for_e = jnp.concatenate(
                [
                    placed((scaled_q * shift).astype(jnp.bfloat16), side),
                    placed((do_t[rows] * factor).astype(jnp.bfloat16), side),
                ],
                axis=0,
            )
            from_e = matmul(e_ref[side], for_e, 1, 1)
            from_u = matmul(u_ref[side], placed(scaled_q.astype(jnp.bfloat16), side), 1, 1)
            k_part = from_e[:, : 2 * HD] + from_u
            v_part = from_e[:, 2 * HD :]
            k_total = k_part if k_total is None else k_total + k_part
            v_total = v_part if v_total is None else v_total + v_part
    out_k[...] = k_total.astype(out_k.dtype)
    out_v[...] = v_total.astype(out_v.dtype)


def key_terms(entries, dtype):
    heads, keys, rows = entries[0][0].shape
    steps = heads // 2
    operands = []
    in_specs = []
    for e, u, query_grad, pair, mine, other in entries:
        operands += [e, u, query_grad, query_grad, pair, mine, other]
        in_specs += [
            per_head_spec(keys, rows),
            per_head_spec(keys, rows),
            column_spec(rows, 0),
            column_spec(rows, steps),
            stat_rows(rows),
            stat_rows(rows),
            stat_rows(rows),
        ]
    return pl.pallas_call(
        key_kernel,
        grid=(steps,),
        in_specs=in_specs,
        out_specs=[column_spec(keys, 0), column_spec(keys, 0)],
        out_shape=[jax.ShapeDtypeStruct((keys, heads * HD), dtype)] * 2,
        name="key_terms",
        compiler_params=pltpu.CompilerParams(vmem_limit_bytes=VMEM_LIMIT),
        cost_estimate=pl.CostEstimate(
            flops=len(entries) * 6 * heads * HD * rows * keys,
            transcendentals=0,
            bytes_accessed=len(entries) * 4 * heads * rows * keys,
        ),
    )(*operands)


def query_kernel(final, acc, mine, other, *refs):
    if final:
        far_o, far_q, out_o, out_q = refs
    else:
        out_o, out_q = refs
    scale = 1.0 / math.sqrt(HD)
    outs = []
    grads = []
    for side in range(2):
        top, inverse, mean = joined(mine, other, side)
        factor = jnp.exp2(mine[0, 3 * side : 3 * side + 1] - top) * inverse
        outs.append(acc[side, :HD] * factor)
        grads.append((acc[side, 2 * HD :] - acc[side, HD : 2 * HD] * mean) * (factor * scale))
    out_rows = jnp.concatenate(outs, axis=0).T
    grad_rows = jnp.concatenate(grads, axis=0).T
    if final:
        out_rows = out_rows + far_o[...].astype(jnp.float32)
        grad_rows = grad_rows + far_q[...].astype(jnp.float32)
    out_o[...] = out_rows.astype(out_o.dtype)
    out_q[...] = grad_rows.astype(out_q.dtype)


def query_terms(acc, mine, other, far):
    heads, _, rows = acc.shape
    steps = heads // 2
    final = far is not None
    extra = list(far) if final else []
    return pl.pallas_call(
        lambda *refs: query_kernel(final, *refs),
        grid=(steps,),
        in_specs=[per_head_spec(3 * HD, rows), stat_rows(rows), stat_rows(rows)]
        + [column_spec(rows, 0)] * len(extra),
        out_specs=[column_spec(rows, 0), column_spec(rows, 0)],
        out_shape=[jax.ShapeDtypeStruct((rows, heads * HD), jnp.bfloat16)] * 2,
        name="query_final" if final else "query_send",
        compiler_params=pltpu.CompilerParams(vmem_limit_bytes=VMEM_LIMIT),
        cost_estimate=pl.CostEstimate(
            flops=8 * heads * HD * rows, transcendentals=0, bytes_accessed=16 * heads * HD * rows
        ),
    )(acc, mine, other, *extra)


def swapped(x, offset):
    devices = lax.axis_size("seq")
    return lax.ppermute(x, "seq", [(i, i ^ offset) for i in range(devices)])


def dense_local(queries, key_states, value_states, grad_output, partners, global_blocks):
    devices = lax.axis_size("seq")
    far = devices // 2
    key_value = jnp.concatenate([key_states, value_states], axis=1)
    query_grad = jnp.concatenate([queries, grad_output], axis=1)
    offsets = list(range(far))
    key_blocks = [key_value]
    for o in offsets[1:]:
        last = o & -o
        key_blocks.append(swapped(key_blocks[o - last], last))
    query_blocks = [query_grad, swapped(query_grad, far)]
    running = [None, None]
    saved = {}
    for at in [(0, k) for k in offsets] + [(1, k) for k in offsets]:
        q, k = at
        moves = (q * far, offsets[k])
        e, u, acc, run, pair = pair_terms(
            (partners, global_blocks), moves, query_blocks[q], key_blocks[k], running[q]
        )
        running[q] = (acc, run)
        saved[at] = (e, u, query_blocks[q], pair)
    others = [swapped(running[1][1], far), swapped(running[0][1], far)]
    sent = query_terms(running[1][0], running[1][1], others[1], None)
    came = [swapped(x, far) for x in sent]
    key_parts = []
    for k in reversed(offsets):
        entries = [saved[(q, k)] + (running[q][1], others[q]) for q in range(2)]
        parts = key_terms(entries, jnp.float32 if k == 0 else jnp.bfloat16)
        key_parts.append(parts if k == 0 else [swapped(x, offsets[k]) for x in parts])
    attended, grad_queries = query_terms(running[0][0], running[0][1], others[0], came)
    grads = [
        sum(parts[i].astype(jnp.float32) for parts in key_parts).astype(jnp.bfloat16)
        for i in range(2)
    ]
    return (attended, grad_queries, grads[0], grads[1])


def local(*operands):
    devices = lax.axis_size("seq")
    paired = devices >= 4 and devices & (devices - 1) == 0
    return (dense_local if paired and devices <= LISTED else routed_local)(*operands)


def solution(mesh):
    in_specs = (
        P(("batch", "seq"), None),
        P(("batch", "seq"), None),
        P(("batch", "seq"), None),
        P(("batch", "seq"), None),
        P("batch", None),
        P("batch"),
    )
    out_specs = (
        P(("batch", "seq"), None),
        P(("batch", "seq"), None),
        P(("batch", "seq"), None),
        P(("batch", "seq"), None),
    )
    return jax.shard_map(local, mesh=mesh, in_specs=in_specs, out_specs=out_specs, check_vma=False)
```

```python
import math

import jax
import jax.numpy as jnp
from jax import lax
from jax.experimental import pallas as pl
from jax.experimental.pallas import tpu as pltpu
from jax.sharding import PartitionSpec as P

HEADS = 6
HD = 64


def extended(x, sides, width):
    for axis, dim in sides:
        devices, length = (lax.axis_size(axis), x.shape[dim])
        up = [(i, (i + 1) % devices) for i in range(devices)]
        down = [(j, i) for i, j in up]
        last = lax.slice_in_dim(x, length - width, length, axis=dim)
        first = lax.slice_in_dim(x, 0, width, axis=dim)
        before = lax.ppermute(last, axis, up)
        after = lax.ppermute(first, axis, down)
        x = jnp.concatenate([before, x, after], axis=dim)
    return x


def from_behind(x, axis, by):
    devices = lax.axis_size(axis)
    return lax.ppermute(x, axis, [(i, (i + by) % devices) for i in range(devices)])


def head_split(matrix):
    return matrix.reshape(matrix.shape[0], HEADS, HD).transpose(1, 0, 2)


def head_join(stacked):
    return stacked.transpose(1, 0, 2).reshape(stacked.shape[1], HEADS * HD)


def attend(queries, key_rows, grad_output):
    features = queries.shape[1]
    scale = 1.0 / math.sqrt(HD)
    contract_last = (((1,), (1,)), ((), ()))
    contract_first = (((0,), (0,)), ((), ()))

    def per_head(head_items):
        query_head, key_head, value_head, grad_head = head_items
        scores = (
            lax.dot_general(query_head, key_head, contract_last, preferred_element_type=jnp.float32)
            * scale
        )
        row_peak = jnp.max(scores, axis=-1, keepdims=True)
        exponent = jnp.exp(scores - row_peak)
        weights = exponent / jnp.sum(exponent, axis=-1, keepdims=True)
        weights_low = weights.astype(jnp.bfloat16)
        output_head = jnp.dot(weights_low, value_head, preferred_element_type=jnp.float32).astype(
            jnp.bfloat16
        )
        grad_weights = lax.dot_general(
            grad_head, value_head, contract_last, preferred_element_type=jnp.float32
        )
        row_dots = jnp.sum(weights * grad_weights, axis=-1, keepdims=True)
        grad_scores = (weights * (grad_weights - row_dots) * scale).astype(jnp.bfloat16)
        grad_query = jnp.dot(grad_scores, key_head, preferred_element_type=jnp.float32).astype(
            jnp.bfloat16
        )
        grad_key = lax.dot_general(
            grad_scores, query_head, contract_first, preferred_element_type=jnp.float32
        )
        grad_value = lax.dot_general(
            weights_low, grad_head, contract_first, preferred_element_type=jnp.float32
        )
        return (output_head, grad_query, grad_key, grad_value)

    outputs, grad_query, grad_key, grad_value = lax.map(
        per_head,
        (
            head_split(queries),
            head_split(key_rows[:, :features]),
            head_split(key_rows[:, features:]),
            head_split(grad_output),
        ),
    )
    grad_pair = jnp.concatenate([head_join(grad_key), head_join(grad_value)], axis=1)
    return (head_join(outputs), head_join(grad_query), grad_pair)


def route_forward(key_value, route_table, devices):
    block_rows, columns = key_value.shape
    pieces = key_value.reshape(devices, block_rows // devices, columns)
    spread = lax.all_to_all(pieces, "seq", split_axis=0, concat_axis=0, tiled=True)
    picked = jnp.take(spread, route_table, axis=0)
    arrived = lax.all_to_all(picked, "seq", split_axis=1, concat_axis=1, tiled=True)
    return arrived.reshape(route_table.shape[0], block_rows, columns)


def route_back(grad_terms, route_table, devices):
    routes, block_rows, columns = grad_terms.shape
    piece_rows = block_rows // devices
    pieces = grad_terms.reshape(routes, devices, piece_rows, columns)
    coming = lax.all_to_all(pieces, "seq", split_axis=1, concat_axis=1, tiled=True)
    block_ids = jnp.arange(devices, dtype=jnp.int32)
    one_hot = (route_table[:, :, None] == block_ids[None, None, :]).astype(jnp.float32)
    summed = jnp.einsum(
        "rds,rdx->sx",
        one_hot,
        coming.reshape(routes, devices, piece_rows * columns),
        precision=lax.Precision.HIGHEST,
    )
    returned = lax.all_to_all(
        summed.reshape(devices, piece_rows, columns), "seq", split_axis=0, concat_axis=0, tiled=True
    )
    return returned.reshape(block_rows, columns)


def routed_local(queries, key_states, value_states, grad_output, partners, global_blocks):
    devices = lax.axis_size("seq")
    block_rows = queries.shape[0]
    features = queries.shape[1]
    key_value = jnp.concatenate([key_states, value_states], axis=1)
    table_rows = []
    table_rows = table_rows + [partners[0], partners[1], partners[2]]
    table_rows = table_rows + [
        jnp.full((devices,), global_blocks[0], jnp.int32),
        jnp.full((devices,), global_blocks[1], jnp.int32),
    ]
    route_table = jnp.stack(table_rows)
    fetched = route_forward(key_value, route_table, devices)
    padded = extended(key_value, (("seq", 0),), block_rows)
    left_block = padded[:block_rows]
    right_block = padded[2 * block_rows :]
    offset = 0
    random_blocks = [fetched[offset], fetched[offset + 1], fetched[offset + 2]]
    global_rows = [fetched[offset + 3], fetched[offset + 4]]
    key_rows = jnp.concatenate(
        [key_value, left_block, right_block] + random_blocks + global_rows, axis=0
    )
    attended, grad_queries, grad_pair = attend(queries, key_rows, grad_output)
    grad_parts = grad_pair.reshape(8, block_rows, 2 * features)
    grad_total = grad_parts[0]
    returning = []
    grad_total = grad_total + from_behind(grad_parts[1], "seq", -1)
    grad_total = grad_total + from_behind(grad_parts[2], "seq", 1)
    returning = returning + [grad_parts[3], grad_parts[4], grad_parts[5]]
    returning = returning + [grad_parts[6], grad_parts[7]]
    grad_total = grad_total + route_back(jnp.stack(returning), route_table, devices)
    return (
        attended,
        grad_queries,
        grad_total[:, :features].astype(jnp.bfloat16),
        grad_total[:, features:].astype(jnp.bfloat16),
    )


LISTED = 8
TO_LOG2 = 1.0 / (math.log(2.0) * math.sqrt(HD))
VMEM_LIMIT = 60 * 1024 * 1024
CHUNK = 256


def matmul(a, b, contract_a, contract_b):
    return lax.dot_general(
        a, b, (((contract_a,), (contract_b,)), ((), ())), preferred_element_type=jnp.float32
    )


def placed(rows, side):
    blank = jnp.zeros_like(rows)
    return jnp.concatenate([rows, blank] if side == 0 else [blank, rows], axis=0)


def listed_times(partners_ref, globals_ref, query_block, key_block, devices):
    count = jnp.int32(0)
    entries = [query_block, lax.rem(query_block + devices - 1, devices)]
    entries += [lax.rem(query_block + 1, devices)]
    entries += [partners_ref[r, query_block] for r in range(partners_ref.shape[0])]
    entries += [globals_ref[g] for g in range(globals_ref.shape[0])]
    for entry in entries:
        count = count + jnp.where(entry == key_block, 1, 0)
    return count


def pair_kernel(first, moves, partners_ref, globals_ref, q_ref, do_ref, k_ref, v_ref, *refs):
    if first:
        e_ref, u_ref, acc_out, run_out, pair_out = refs
    else:
        acc_in, run_in, e_ref, u_ref, acc_out, run_out, pair_out = refs
    devices = lax.axis_size("seq")
    me = lax.axis_index("seq")
    count = listed_times(
        partners_ref, globals_ref, me ^ moves[0], me ^ moves[1], devices
    ).astype(jnp.float32)
    bias = jnp.log2(jnp.full((1, CHUNK), jnp.maximum(count, 1.0), jnp.float32))
    bias = jnp.where(count > 0.0, bias, -1e30)
    keys = k_ref[...]
    values = v_ref[...]
    keys_twice = jnp.concatenate([keys, keys], axis=1)
    q_t = q_ref[...].T.astype(jnp.float32) * TO_LOG2
    q_high = q_t.astype(jnp.bfloat16)
    q_low = (q_t - q_high.astype(jnp.float32)).astype(jnp.bfloat16)
    do_t = do_ref[...].T
    k_t = keys.T
    v_t = values.T
    ones = jnp.ones((16, keys.shape[0]), jnp.bfloat16)
    units = [(side, at) for side in range(2) for at in range(q_ref.shape[0] // CHUNK)]
    halves = [slice(0, HD), slice(HD, 2 * HD)]
    lanes = [slice(at * CHUNK, (at + 1) * CHUNK) for at in range(q_ref.shape[0] // CHUNK)]
    state = [{} for _ in units]

    def products(n):
        side, at = units[n]
        rows, cols = halves[side], lanes[at]
        both_q = [placed(q_high[rows, cols], side), placed(q_low[rows, cols], side)]
        state[n]["scores"] = matmul(keys_twice, jnp.concatenate(both_q, axis=0), 1, 0)

    def exponents(n):
        side, at = units[n]
        scores = state[n].pop("scores")
        peak = jnp.max(scores, axis=0, keepdims=True)
        low = jnp.exp2(scores - peak).astype(jnp.bfloat16)
        e_ref[side, :, lanes[at]] = low
        state[n]["peak"] = peak
        state[n]["low"] = low

    def sums(n):
        side, at = units[n]
        rows = halves[side]
        left = jnp.concatenate([v_t[rows], k_t[rows], ones], axis=0)
        state[n]["both"] = matmul(left, state[n]["low"], 1, 0)

    def centre(n):
        side, at = units[n]
        both = state[n]["both"]
        total = both[2 * HD : 2 * HD + 1]
        left = do_t[halves[side], lanes[at]].astype(jnp.float32)
        dots = jnp.sum(both[:HD] * left, axis=0, keepdims=True)
        mean = dots / total
        grad = matmul(values, placed(do_t[halves[side], lanes[at]], side), 1, 0)
        centred = state[n].pop("low") * (grad - mean).astype(jnp.bfloat16)
        u_ref[side, :, lanes[at]] = centred
        state[n].update(total=total, dots=dots, mean=mean, centred=centred)

    def finish(n):
        side, at = units[n]
        cols = lanes[at]
        one = state[n]
        both = one["both"]
        moved = matmul(k_t[halves[side]], one["centred"], 1, 0) + one["mean"] * both[HD : 2 * HD]
        peak = one["peak"] + bias
        if first:
            acc_out[side, : 2 * HD, cols] = both[: 2 * HD]
            acc_out[side, 2 * HD :, cols] = moved
            top, total, dots = peak, one["total"], one["dots"]
        else:
            at_row = 3 * side
            old = run_in[0, at_row : at_row + 1, cols]
            top = jnp.maximum(old, peak)
            keep = jnp.exp2(old - top)
            take = jnp.exp2(peak - top)
            acc_out[side, : 2 * HD, cols] = (
                acc_in[side, : 2 * HD, cols] * keep + both[: 2 * HD] * take
            )
            acc_out[side, 2 * HD :, cols] = acc_in[side, 2 * HD :, cols] * keep + moved * take
            total = run_in[0, at_row + 1 : at_row + 2, cols] * keep + one["total"] * take
            dots = run_in[0, at_row + 2 : at_row + 3, cols] * keep + one["dots"] * take
        for row, value in enumerate((top, total, dots)):
            run_out[0, 3 * side + row : 3 * side + row + 1, cols] = value
        for row, value in enumerate((peak, one["mean"])):
            pair_out[0, 3 * side + row : 3 * side + row + 1, cols] = value
        state[n].clear()

    last = len(units) - 1
    products(0)
    products(1)
    for n in range(len(units)):
        exponents(n)
        sums(n)
        if n + 2 <= last:
            products(n + 2)
        if n >= 1:
            centre(n - 1)
            finish(n - 1)
    centre(last)
    finish(last)


def head_pairs(features):
    return features // (2 * HD)


def column_spec(rows, offset):
    return pl.BlockSpec((rows, 2 * HD), lambda p: (0, p + offset))


def per_head_spec(*tail):
    return pl.BlockSpec((2,) + tail, lambda p: (p,) + (0,) * len(tail))


def stat_rows(rows):
    return pl.BlockSpec((1, 8, rows), lambda p: (p, 0, 0))


def pair_terms(tables, moves, query_grad, key_value, running):
    rows, columns = query_grad.shape
    keys = key_value.shape[0]
    features = columns // 2
    steps = head_pairs(features)
    heads = 2 * steps
    first = running is None
    state = [] if first else list(running)
    acc = jax.ShapeDtypeStruct((heads, 3 * HD, rows), jnp.float32)
    stat = jax.ShapeDtypeStruct((steps, 8, rows), jnp.float32)
    big = jax.ShapeDtypeStruct((heads, keys, rows), jnp.bfloat16)
    acc_spec = per_head_spec(3 * HD, rows)
    stat_spec = stat_rows(rows)
    big_spec = per_head_spec(keys, rows)
    return pl.pallas_call(
        lambda *refs: pair_kernel(first, moves, *refs),
        grid=(steps,),
        in_specs=[
            pl.BlockSpec(memory_space=pltpu.SMEM),
            pl.BlockSpec(memory_space=pltpu.SMEM),
            column_spec(rows, 0),
            column_spec(rows, steps),
            column_spec(keys, 0),
            column_spec(keys, steps),
        ]
        + ([] if first else [acc_spec, stat_spec]),
        out_specs=[big_spec, big_spec, acc_spec, stat_spec, stat_spec],
        out_shape=[big, big, acc, stat, stat],
        name="pair_first" if first else "pair_next",
        compiler_params=pltpu.CompilerParams(vmem_limit_bytes=VMEM_LIMIT),
        cost_estimate=pl.CostEstimate(
            flops=8 * heads * HD * rows * keys,
            transcendentals=heads * rows * keys,
            bytes_accessed=4 * heads * rows * keys,
        ),
    )(*tables, query_grad, query_grad, key_value, key_value, *state)


def joined(mine, other, side):
    at = 3 * side
    top = jnp.maximum(mine[0, at : at + 1], other[0, at : at + 1])
    here = jnp.exp2(mine[0, at : at + 1] - top)
    there = jnp.exp2(other[0, at : at + 1] - top)
    inverse = 1.0 / (mine[0, at + 1 : at + 2] * here + other[0, at + 1 : at + 2] * there)
    mean = (mine[0, at + 2 : at + 3] * here + other[0, at + 2 : at + 3] * there) * inverse
    return top, inverse, mean


def key_kernel(*refs):
    out_k, out_v = refs[-2:]
    scale = 1.0 / math.sqrt(HD)
    k_total = None
    v_total = None
    for at in range(0, len(refs) - 2, 7):
        e_ref, u_ref, q_ref, do_ref, pair_ref, mine, other = refs[at : at + 7]
        q_t = q_ref[...].T.astype(jnp.float32)
        do_t = do_ref[...].T.astype(jnp.float32)
        for side in range(2):
            rows = slice(side * HD, (side + 1) * HD)
            top, inverse, mean = joined(mine, other, side)
            factor = jnp.exp2(pair_ref[0, 3 * side : 3 * side + 1] - top) * inverse
            shift = pair_ref[0, 3 * side + 1 : 3 * side + 2] - mean
            scaled_q = q_t[rows] * (factor * scale)
            for_e = jnp.concatenate(
                [
                    placed((scaled_q * shift).astype(jnp.bfloat16), side),
                    placed((do_t[rows] * factor).astype(jnp.bfloat16), side),
                ],
                axis=0,
            )
            from_e = matmul(e_ref[side], for_e, 1, 1)
            from_u = matmul(u_ref[side], placed(scaled_q.astype(jnp.bfloat16), side), 1, 1)
            k_part = from_e[:, : 2 * HD] + from_u
            v_part = from_e[:, 2 * HD :]
            k_total = k_part if k_total is None else k_total + k_part
            v_total = v_part if v_total is None else v_total + v_part
    out_k[...] = k_total.astype(out_k.dtype)
    out_v[...] = v_total.astype(out_v.dtype)


def key_terms(entries, dtype):
    heads, keys, rows = entries[0][0].shape
    steps = heads // 2
    operands = []
    in_specs = []
    for e, u, query_grad, pair, mine, other in entries:
        operands += [e, u, query_grad, query_grad, pair, mine, other]
        in_specs += [
            per_head_spec(keys, rows),
            per_head_spec(keys, rows),
            column_spec(rows, 0),
            column_spec(rows, steps),
            stat_rows(rows),
            stat_rows(rows),
            stat_rows(rows),
        ]
    return pl.pallas_call(
        key_kernel,
        grid=(steps,),
        in_specs=in_specs,
        out_specs=[column_spec(keys, 0), column_spec(keys, 0)],
        out_shape=[jax.ShapeDtypeStruct((keys, heads * HD), dtype)] * 2,
        name="key_terms",
        compiler_params=pltpu.CompilerParams(vmem_limit_bytes=VMEM_LIMIT),
        cost_estimate=pl.CostEstimate(
            flops=len(entries) * 6 * heads * HD * rows * keys,
            transcendentals=0,
            bytes_accessed=len(entries) * 4 * heads * rows * keys,
        ),
    )(*operands)


def query_kernel(final, acc, mine, other, *refs):
    if final:
        far_o, far_q, out_o, out_q = refs
    else:
        out_o, out_q = refs
    scale = 1.0 / math.sqrt(HD)
    outs = []
    grads = []
    for side in range(2):
        top, inverse, mean = joined(mine, other, side)
        factor = jnp.exp2(mine[0, 3 * side : 3 * side + 1] - top) * inverse
        outs.append(acc[side, :HD] * factor)
        grads.append((acc[side, 2 * HD :] - acc[side, HD : 2 * HD] * mean) * (factor * scale))
    out_rows = jnp.concatenate(outs, axis=0).T
    grad_rows = jnp.concatenate(grads, axis=0).T
    if final:
        out_rows = out_rows + far_o[...].astype(jnp.float32)
        grad_rows = grad_rows + far_q[...].astype(jnp.float32)
    out_o[...] = out_rows.astype(out_o.dtype)
    out_q[...] = grad_rows.astype(out_q.dtype)


def query_terms(acc, mine, other, far):
    heads, _, rows = acc.shape
    steps = heads // 2
    final = far is not None
    extra = list(far) if final else []
    return pl.pallas_call(
        lambda *refs: query_kernel(final, *refs),
        grid=(steps,),
        in_specs=[per_head_spec(3 * HD, rows), stat_rows(rows), stat_rows(rows)]
        + [column_spec(rows, 0)] * len(extra),
        out_specs=[column_spec(rows, 0), column_spec(rows, 0)],
        out_shape=[jax.ShapeDtypeStruct((rows, heads * HD), jnp.bfloat16)] * 2,
        name="query_final" if final else "query_send",
        compiler_params=pltpu.CompilerParams(vmem_limit_bytes=VMEM_LIMIT),
        cost_estimate=pl.CostEstimate(
            flops=8 * heads * HD * rows, transcendentals=0, bytes_accessed=16 * heads * HD * rows
        ),
    )(acc, mine, other, *extra)


def swapped(x, offset):
    devices = lax.axis_size("seq")
    return lax.ppermute(x, "seq", [(i, i ^ offset) for i in range(devices)])


def pack_kernel(k_ref, v_ref, q_ref, do_ref, kv_ref, qd_ref):
    features = k_ref.shape[1]
    qd_ref[:, :features] = q_ref[...]
    qd_ref[:, features:] = do_ref[...]
    kv_ref[:, :features] = k_ref[...]
    kv_ref[:, features:] = v_ref[...]


def packed(key_states, value_states, queries, grad_output):
    rows, features = queries.shape
    both = jax.ShapeDtypeStruct((rows, 2 * features), queries.dtype)
    whole = pl.BlockSpec(memory_space=pltpu.VMEM)
    return pl.pallas_call(
        pack_kernel,
        in_specs=[whole] * 4,
        out_specs=[whole] * 2,
        out_shape=[both, both],
        name="pack",
    )(key_states, value_states, queries, grad_output)


def after(x, earlier):
    return lax.optimization_barrier((x, earlier))[0]


def dense_local(queries, key_states, value_states, grad_output, partners, global_blocks):
    devices = lax.axis_size("seq")
    far = devices // 2
    tables = (partners, global_blocks)
    key_value, query_grad = packed(key_states, value_states, queries, grad_output)
    query_blocks = [query_grad, swapped(query_grad, far)]
    offsets = list(range(far))
    key_blocks = {0: key_value}
    running = [None, None]
    saved = {}
    order = [None]

    def pair(q, k):
        query_block = query_blocks[q]
        if order[0] is not None:
            query_block = after(query_block, order[0])
        e, u, acc, run, stat = pair_terms(
            tables, (q * far, k), query_block, key_blocks[k], running[q]
        )
        running[q] = (acc, run)
        saved[(q, k)] = (e, u, query_blocks[q], stat)
        order[0] = stat

    neighbours = [o for o in offsets if o and o & (o - 1) == 0]
    for o in neighbours:
        key_blocks[o] = swapped(key_value, o)
    pair(0, 0)
    relayed = [o for o in offsets if o and o not in neighbours]
    for o in neighbours[:-1]:
        pair(0, o)
    for o in relayed:
        last = o & -o
        key_blocks[o] = swapped(after(key_blocks[o - last], order[0]), last)
    pair(0, neighbours[-1])
    for o in [0] + neighbours:
        pair(1, o)
    for o in relayed:
        pair(1, o)
    others = {0: swapped(running[1][1], far)}
    for o in relayed:
        pair(0, o)
    others[1] = swapped(running[0][1], far)
    sent = query_terms(running[1][0], running[1][1], others[1], None)
    came = [swapped(x, far) for x in sent]
    key_parts = []
    for k in reversed(offsets):
        entries = [saved[(q, k)] + (running[q][1], others[q]) for q in range(2)]
        parts = key_terms(entries, jnp.float32 if k == 0 else jnp.bfloat16)
        key_parts.append(parts if k == 0 else [swapped(x, k) for x in parts])
    came = [after(x, key_parts[-1][0]) for x in came]
    attended, grad_queries = query_terms(running[0][0], running[0][1], others[0], came)
    grads = [
        sum(parts[i].astype(jnp.float32) for parts in key_parts).astype(jnp.bfloat16)
        for i in range(2)
    ]
    return (attended, grad_queries, grads[0], grads[1])


def local(*operands):
    devices = lax.axis_size("seq")
    paired = devices >= 4 and devices & (devices - 1) == 0
    return (dense_local if paired and devices <= LISTED else routed_local)(*operands)


def solution(mesh):
    in_specs = (
        P(("batch", "seq"), None),
        P(("batch", "seq"), None),
        P(("batch", "seq"), None),
        P(("batch", "seq"), None),
        P("batch", None),
        P("batch"),
    )
    out_specs = (
        P(("batch", "seq"), None),
        P(("batch", "seq"), None),
        P(("batch", "seq"), None),
        P(("batch", "seq"), None),
    )
    return jax.shard_map(local, mesh=mesh, in_specs=in_specs, out_specs=out_specs, check_vma=False)
```

```python
import math

import jax
import jax.numpy as jnp
from jax import lax
from jax.experimental import pallas as pl
from jax.experimental.pallas import tpu as pltpu
from jax.sharding import PartitionSpec as P

HEADS = 6
HD = 64


def extended(x, sides, width):
    for axis, dim in sides:
        devices, length = (lax.axis_size(axis), x.shape[dim])
        up = [(i, (i + 1) % devices) for i in range(devices)]
        down = [(j, i) for i, j in up]
        last = lax.slice_in_dim(x, length - width, length, axis=dim)
        first = lax.slice_in_dim(x, 0, width, axis=dim)
        before = lax.ppermute(last, axis, up)
        after = lax.ppermute(first, axis, down)
        x = jnp.concatenate([before, x, after], axis=dim)
    return x


def from_behind(x, axis, by):
    devices = lax.axis_size(axis)
    return lax.ppermute(x, axis, [(i, (i + by) % devices) for i in range(devices)])


def head_split(matrix):
    return matrix.reshape(matrix.shape[0], HEADS, HD).transpose(1, 0, 2)


def head_join(stacked):
    return stacked.transpose(1, 0, 2).reshape(stacked.shape[1], HEADS * HD)


def attend(queries, key_rows, grad_output):
    features = queries.shape[1]
    scale = 1.0 / math.sqrt(HD)
    contract_last = (((1,), (1,)), ((), ()))
    contract_first = (((0,), (0,)), ((), ()))

    def per_head(head_items):
        query_head, key_head, value_head, grad_head = head_items
        scores = (
            lax.dot_general(query_head, key_head, contract_last, preferred_element_type=jnp.float32)
            * scale
        )
        row_peak = jnp.max(scores, axis=-1, keepdims=True)
        exponent = jnp.exp(scores - row_peak)
        weights = exponent / jnp.sum(exponent, axis=-1, keepdims=True)
        weights_low = weights.astype(jnp.bfloat16)
        output_head = jnp.dot(weights_low, value_head, preferred_element_type=jnp.float32).astype(
            jnp.bfloat16
        )
        grad_weights = lax.dot_general(
            grad_head, value_head, contract_last, preferred_element_type=jnp.float32
        )
        row_dots = jnp.sum(weights * grad_weights, axis=-1, keepdims=True)
        grad_scores = (weights * (grad_weights - row_dots) * scale).astype(jnp.bfloat16)
        grad_query = jnp.dot(grad_scores, key_head, preferred_element_type=jnp.float32).astype(
            jnp.bfloat16
        )
        grad_key = lax.dot_general(
            grad_scores, query_head, contract_first, preferred_element_type=jnp.float32
        )
        grad_value = lax.dot_general(
            weights_low, grad_head, contract_first, preferred_element_type=jnp.float32
        )
        return (output_head, grad_query, grad_key, grad_value)

    outputs, grad_query, grad_key, grad_value = lax.map(
        per_head,
        (
            head_split(queries),
            head_split(key_rows[:, :features]),
            head_split(key_rows[:, features:]),
            head_split(grad_output),
        ),
    )
    grad_pair = jnp.concatenate([head_join(grad_key), head_join(grad_value)], axis=1)
    return (head_join(outputs), head_join(grad_query), grad_pair)


def route_forward(key_value, route_table, devices):
    block_rows, columns = key_value.shape
    pieces = key_value.reshape(devices, block_rows // devices, columns)
    spread = lax.all_to_all(pieces, "seq", split_axis=0, concat_axis=0, tiled=True)
    picked = jnp.take(spread, route_table, axis=0)
    arrived = lax.all_to_all(picked, "seq", split_axis=1, concat_axis=1, tiled=True)
    return arrived.reshape(route_table.shape[0], block_rows, columns)


def route_back(grad_terms, route_table, devices):
    routes, block_rows, columns = grad_terms.shape
    piece_rows = block_rows // devices
    pieces = grad_terms.reshape(routes, devices, piece_rows, columns)
    coming = lax.all_to_all(pieces, "seq", split_axis=1, concat_axis=1, tiled=True)
    block_ids = jnp.arange(devices, dtype=jnp.int32)
    one_hot = (route_table[:, :, None] == block_ids[None, None, :]).astype(jnp.float32)
    summed = jnp.einsum(
        "rds,rdx->sx",
        one_hot,
        coming.reshape(routes, devices, piece_rows * columns),
        precision=lax.Precision.HIGHEST,
    )
    returned = lax.all_to_all(
        summed.reshape(devices, piece_rows, columns), "seq", split_axis=0, concat_axis=0, tiled=True
    )
    return returned.reshape(block_rows, columns)


def routed_local(queries, key_states, value_states, grad_output, partners, global_blocks):
    devices = lax.axis_size("seq")
    block_rows = queries.shape[0]
    features = queries.shape[1]
    key_value = jnp.concatenate([key_states, value_states], axis=1)
    table_rows = []
    table_rows = table_rows + [partners[0], partners[1], partners[2]]
    table_rows = table_rows + [
        jnp.full((devices,), global_blocks[0], jnp.int32),
        jnp.full((devices,), global_blocks[1], jnp.int32),
    ]
    route_table = jnp.stack(table_rows)
    fetched = route_forward(key_value, route_table, devices)
    padded = extended(key_value, (("seq", 0),), block_rows)
    left_block = padded[:block_rows]
    right_block = padded[2 * block_rows :]
    offset = 0
    random_blocks = [fetched[offset], fetched[offset + 1], fetched[offset + 2]]
    global_rows = [fetched[offset + 3], fetched[offset + 4]]
    key_rows = jnp.concatenate(
        [key_value, left_block, right_block] + random_blocks + global_rows, axis=0
    )
    attended, grad_queries, grad_pair = attend(queries, key_rows, grad_output)
    grad_parts = grad_pair.reshape(8, block_rows, 2 * features)
    grad_total = grad_parts[0]
    returning = []
    grad_total = grad_total + from_behind(grad_parts[1], "seq", -1)
    grad_total = grad_total + from_behind(grad_parts[2], "seq", 1)
    returning = returning + [grad_parts[3], grad_parts[4], grad_parts[5]]
    returning = returning + [grad_parts[6], grad_parts[7]]
    grad_total = grad_total + route_back(jnp.stack(returning), route_table, devices)
    return (
        attended,
        grad_queries,
        grad_total[:, :features].astype(jnp.bfloat16),
        grad_total[:, features:].astype(jnp.bfloat16),
    )


ORDER = [
    "p0",
    "c0",
    "p1",
    "e0",
    "c1",
    "f0",
    "s0",
    "p2",
    "e1",
    "c2",
    "s1",
    "p3",
    "e2",
    "c3",
    "f2",
    "s2",
    "f1",
    "e3",
    "f3",
    "s3",
]
LISTED = 8
TO_LOG2 = 1.0 / (math.log(2.0) * math.sqrt(HD))
VMEM_LIMIT = 60 * 1024 * 1024


def matmul(a, b, contract_a, contract_b):
    return lax.dot_general(
        a, b, (((contract_a,), (contract_b,)), ((), ())), preferred_element_type=jnp.float32
    )


def placed(rows, side):
    blank = jnp.zeros_like(rows)
    return jnp.concatenate([rows, blank] if side == 0 else [blank, rows], axis=0)


def listed_times(partners_ref, globals_ref, query_block, key_block, devices):
    count = jnp.int32(0)
    entries = [query_block, lax.rem(query_block + devices - 1, devices)]
    entries += [lax.rem(query_block + 1, devices)]
    entries += [partners_ref[r, query_block] for r in range(partners_ref.shape[0])]
    entries += [globals_ref[g] for g in range(globals_ref.shape[0])]
    for entry in entries:
        count = count + jnp.where(entry == key_block, 1, 0)
    return count


def chosen(index, values):
    result = values[0]
    for at in range(1, len(values)):
        result = jnp.where(index == at, values[at], result)
    return result


def pairs_kernel(plan, partners_ref, globals_ref, *refs):
    pairs, query_moves, key_moves, carried = plan
    queries, keys = len(query_moves), len(key_moves)
    query_refs = refs[: 2 * queries]
    key_refs = refs[2 * queries : 2 * (queries + keys)]
    refs = refs[2 * (queries + keys) :]
    if carried:
        acc_in, run_in = refs[:2]
        refs = refs[2:]
    e_ref, u_ref, acc_ref, run_ref, pair_ref = refs[:5]
    q_now, do_now, k_now, v_now, low_kept, both_kept, peak_kept, v_kept, kt_kept, dt_kept = refs[5:]
    step = pl.program_id(0)
    total_steps = pl.num_programs(0) - 1
    per_pair = total_steps // len(pairs)
    now = jnp.minimum(step, total_steps - 1)
    then = jnp.maximum(step - 1, 0)
    slot, old_slot = lax.rem(step, 2), lax.rem(step + 1, 2)
    pair_now, pair_then = now // per_pair, then // per_pair
    group = lax.rem(then, per_pair)
    for at in range(queries):

        @pl.when(chosen(pair_now, [q for q, _ in pairs]) == at)
        def _():
            q_now[...] = query_refs[2 * at][...]
            do_now[...] = query_refs[2 * at + 1][...]

    for at in range(keys):

        @pl.when(chosen(pair_now, [k for _, k in pairs]) == at)
        def _():
            k_now[...] = key_refs[2 * at][...]
            v_now[...] = key_refs[2 * at + 1][...]

    chunk = q_now.shape[0] // 2
    devices = lax.axis_size("seq")
    me = lax.axis_index("seq")
    count = listed_times(
        partners_ref,
        globals_ref,
        me ^ chosen(pair_then, [query_moves[q] for q, _ in pairs]),
        me ^ chosen(pair_then, [key_moves[k] for _, k in pairs]),
        devices,
    ).astype(jnp.float32)
    bias = jnp.log2(jnp.full((1, chunk), jnp.maximum(count, 1.0), jnp.float32))
    bias = jnp.where(count > 0.0, bias, -1e30)
    member = chosen(pair_then, [q for q, _ in pairs])
    first_head = 2 * group

    key_rows = k_now[...]
    values = v_now[...]
    keys_twice = jnp.concatenate([key_rows, key_rows], axis=1)
    q_t = q_now[...].T.astype(jnp.float32) * TO_LOG2
    q_high = q_t.astype(jnp.bfloat16)
    q_low = (q_t - q_high.astype(jnp.float32)).astype(jnp.bfloat16)
    k_t = key_rows.T
    v_t = values.T
    v_kept[slot] = values
    kt_kept[slot] = k_t
    dt_kept[slot] = do_now[...].T
    ones = jnp.ones((16, key_rows.shape[0]), jnp.bfloat16)
    units = [(side, at) for side in range(2) for at in range(2)]
    halves = [slice(0, HD), slice(HD, 2 * HD)]
    lanes = [slice(at * chunk, (at + 1) * chunk) for at in range(2)]
    scores = {}
    lows = {}
    centred = {}

    def products(n):
        side, at = units[n]
        both_q = [placed(x[halves[side], lanes[at]], side) for x in (q_high, q_low)]
        scores[n] = matmul(keys_twice, jnp.concatenate(both_q, axis=0), 1, 0)

    def exponents(n):
        side, at = units[n]
        peak = jnp.max(scores[n], axis=0, keepdims=True)
        low = jnp.exp2(scores.pop(n) - peak).astype(jnp.bfloat16)
        e_ref[0, side, :, lanes[at]] = low
        low_kept[slot, side, :, lanes[at]] = low
        peak_kept[slot, side : side + 1, lanes[at]] = peak
        lows[n] = low

    def sums(n):
        side, at = units[n]
        left = jnp.concatenate([v_t[halves[side]], k_t[halves[side]], ones], axis=0)
        both_kept[slot, side, :, lanes[at]] = matmul(left, lows.pop(n), 1, 0)

    def centre(n):
        side, at = units[n]
        cols = lanes[at]
        do_t = dt_kept[old_slot, halves[side], cols]
        upper = both_kept[old_slot, side, :HD, cols]
        total = both_kept[old_slot, side, 2 * HD : 2 * HD + 1, cols]
        dots = jnp.sum(upper * do_t.astype(jnp.float32), axis=0, keepdims=True)
        mean = dots / total
        grad = matmul(v_kept[old_slot], placed(do_t, side), 1, 0)
        shifted = low_kept[old_slot, side, :, cols] * (grad - mean).astype(jnp.bfloat16)
        u_ref[0, side, :, cols] = shifted
        centred[n] = (shifted, total, dots, mean)

    def finish(n):
        side, at = units[n]
        cols = lanes[at]
        shifted, total, dots, mean = centred.pop(n)
        both = both_kept[old_slot, side, : 2 * HD, cols]
        moved = matmul(kt_kept[old_slot, halves[side]], shifted, 1, 0) + mean * both[HD:]
        peak = peak_kept[old_slot, side : side + 1, cols] + bias
        head = first_head + side
        row = 3 * side
        old = run_ref[member, group, row : row + 1, cols]
        top = jnp.maximum(old, peak)
        keep = jnp.exp2(old - top)
        take = jnp.exp2(peak - top)
        acc_ref[member, head, : 2 * HD, cols] = (
            acc_ref[member, head, : 2 * HD, cols] * keep + both * take
        )
        acc_ref[member, head, 2 * HD :, cols] = (
            acc_ref[member, head, 2 * HD :, cols] * keep + moved * take
        )
        total = run_ref[member, group, row + 1 : row + 2, cols] * keep + total * take
        dots = run_ref[member, group, row + 2 : row + 3, cols] * keep + dots * take
        for at_row, value in enumerate((top, total, dots)):
            run_ref[member, group, row + at_row : row + at_row + 1, cols] = value
        for at_row, value in enumerate((peak, mean)):
            pair_ref[0, row + at_row : row + at_row + 1, cols] = value

    stages = dict(p=products, e=exponents, s=sums, c=centre, f=finish)
    for name in ORDER:
        stages[name[0]](int(name[1:]))

    @pl.when(step == 0)
    def _():
        acc_ref[...] = jnp.zeros_like(acc_ref)
        run_ref[...] = jnp.zeros_like(run_ref)
        for member_at in range(acc_ref.shape[0]):
            if member_at < carried:
                acc_ref[member_at] = acc_in[member_at]
                run_ref[member_at] = run_in[member_at]
            else:
                for row in (0, 3):
                    shape = (run_ref.shape[1], 1, run_ref.shape[3])
                    run_ref[member_at, :, row : row + 1] = jnp.full(shape, -1e30, jnp.float32)


def head_pairs(features):
    return features // (2 * HD)


def column_spec(rows, offset):
    return pl.BlockSpec((rows, 2 * HD), lambda p: (0, p + offset))


def step_spec(offset, steps, used, last, *block):
    def index(p):
        now = jnp.minimum(p, last)
        live = sum(jnp.where(now // steps == at, 1, 0) for at in used)
        return (0, lax.rem(now, steps) * live + offset)

    return pl.BlockSpec(block, index)


def pair_terms(tables, pairs, query_blocks, key_blocks, running):
    query_moves, query_arrays = zip(*query_blocks)
    key_moves, key_arrays = zip(*key_blocks)
    rows, columns = query_arrays[0].shape
    keys = key_arrays[0].shape[0]
    features = columns // 2
    steps = head_pairs(features)
    heads = 2 * steps
    total = len(pairs) * steps
    members = len(query_arrays)
    state = [] if running is None else list(running)
    carried = state[0].shape[0] if state else 0
    plan = (pairs, query_moves, key_moves, carried)
    acc = jax.ShapeDtypeStruct((members, heads, 3 * HD, rows), jnp.float32)
    run = jax.ShapeDtypeStruct((members, steps, 8, rows), jnp.float32)
    stat = jax.ShapeDtypeStruct((total, 8, rows), jnp.float32)
    big = jax.ShapeDtypeStruct((total, 2, keys, rows), jnp.bfloat16)
    operands = []
    in_specs = [pl.BlockSpec(memory_space=pltpu.SMEM)] * 2
    for kind, arrays in ((0, query_arrays), (1, key_arrays)):
        for which, array in enumerate(arrays):
            used = [at for at, pair in enumerate(pairs) if pair[kind] == which]
            length = array.shape[0]
            in_specs.append(step_spec(0, steps, used, total - 1, length, 2 * HD))
            in_specs.append(step_spec(steps, steps, used, total - 1, length, 2 * HD))
            operands += [array, array]
    whole = pl.BlockSpec(memory_space=pltpu.VMEM)
    in_specs += [whole] * len(state)
    now = lambda p: (jnp.minimum(p, total - 1), 0, 0, 0)
    then = lambda p: (jnp.maximum(p - 1, 0), 0, 0, 0)
    block = (1, 2, keys, rows)
    tile = pltpu.VMEM((rows, 2 * HD), jnp.bfloat16)
    return pl.pallas_call(
        lambda *refs: pairs_kernel(plan, *refs),
        grid=(total + 1,),
        in_specs=in_specs,
        out_specs=[
            pl.BlockSpec(block, now),
            pl.BlockSpec(block, then),
            whole,
            whole,
            pl.BlockSpec((1, 8, rows), lambda p: then(p)[:3]),
        ],
        out_shape=[big, big, acc, run, stat],
        scratch_shapes=[
            tile,
            tile,
            pltpu.VMEM((keys, 2 * HD), jnp.bfloat16),
            pltpu.VMEM((keys, 2 * HD), jnp.bfloat16),
            pltpu.VMEM((2, 2, keys, rows), jnp.bfloat16),
            pltpu.VMEM((2, 2, 2 * HD + 16, rows), jnp.float32),
            pltpu.VMEM((2, 8, rows), jnp.float32),
            pltpu.VMEM((2, keys, 2 * HD), jnp.bfloat16),
            pltpu.VMEM((2, 2 * HD, keys), jnp.bfloat16),
            pltpu.VMEM((2, 2 * HD, rows), jnp.bfloat16),
        ],
        compiler_params=pltpu.CompilerParams(vmem_limit_bytes=VMEM_LIMIT),
        cost_estimate=pl.CostEstimate(
            flops=len(pairs) * 8 * heads * HD * rows * keys,
            transcendentals=len(pairs) * heads * rows * keys,
            bytes_accessed=len(pairs) * 4 * heads * rows * keys,
        ),
    )(*tables, *operands, *state)


def joined(mine, other, side):
    at = 3 * side
    top = jnp.maximum(mine[at : at + 1], other[at : at + 1])
    here = jnp.exp2(mine[at : at + 1] - top)
    there = jnp.exp2(other[at : at + 1] - top)
    inverse = 1.0 / (mine[at + 1 : at + 2] * here + other[at + 1 : at + 2] * there)
    mean = (mine[at + 2 : at + 3] * here + other[at + 2 : at + 3] * there) * inverse
    share = other[at + 1 : at + 2] * there * inverse
    return top, inverse, mean, share


def key_kernel(*refs):
    out = refs[-1]
    features = out.shape[1] // 2
    scale = 1.0 / math.sqrt(HD)
    k_total = None
    v_total = None
    for at in range(0, len(refs) - 1, 7):
        e_ref, u_ref, q_ref, do_ref, pair_ref, mine, other = refs[at : at + 7]
        q_t = q_ref[...].T.astype(jnp.float32)
        do_t = do_ref[...].T.astype(jnp.float32)
        for side in range(2):
            rows = slice(side * HD, (side + 1) * HD)
            top, inverse, mean, _ = joined(mine.at[0, 0], other.at[0, 0], side)
            factor = jnp.exp2(pair_ref[0, 3 * side : 3 * side + 1] - top) * inverse
            shift = pair_ref[0, 3 * side + 1 : 3 * side + 2] - mean
            scaled_q = q_t[rows] * (factor * scale)
            for_e = jnp.concatenate(
                [
                    placed((scaled_q * shift).astype(jnp.bfloat16), side),
                    placed((do_t[rows] * factor).astype(jnp.bfloat16), side),
                ],
                axis=0,
            )
            from_e = matmul(e_ref[0, side], for_e, 1, 1)
            from_u = matmul(u_ref[0, side], placed(scaled_q.astype(jnp.bfloat16), side), 1, 1)
            k_part = from_e[:, : 2 * HD] + from_u
            v_part = from_e[:, 2 * HD :]
            k_total = k_part if k_total is None else k_total + k_part
            v_total = v_part if v_total is None else v_total + v_part
    at = pl.program_id(0) * (2 * HD)
    out[:, pl.ds(pl.multiple_of(at, 2 * HD), 2 * HD)] = k_total.astype(out.dtype)
    at = at + features
    out[:, pl.ds(pl.multiple_of(at, 2 * HD), 2 * HD)] = v_total.astype(out.dtype)


def member_rows(member, rows):
    return pl.BlockSpec((1, 1, 8, rows), lambda p: (member, p, 0, 0))


def key_terms(entries, mine, theirs, dtype):
    operands = []
    in_specs = []
    for member, (e, u, query_grad, stat, base) in enumerate(entries):
        _, _, keys, rows = e.shape
        steps = head_pairs(query_grad.shape[1] // 2)
        block = pl.BlockSpec((1, 2, keys, rows), lambda p, base=base: (p + base, 0, 0, 0))
        operands += [e, u, query_grad, query_grad, stat, mine, theirs]
        in_specs += [
            block,
            block,
            column_spec(rows, 0),
            column_spec(rows, steps),
            pl.BlockSpec((1, 8, rows), lambda p, base=base: (p + base, 0, 0)),
            member_rows(member, rows),
            member_rows(1 - member, rows),
        ]
    heads = 2 * steps
    return pl.pallas_call(
        key_kernel,
        grid=(steps,),
        in_specs=in_specs,
        out_specs=pl.BlockSpec(memory_space=pltpu.VMEM),
        out_shape=jax.ShapeDtypeStruct((keys, 2 * heads * HD), dtype),
        name="key_terms",
        compiler_params=pltpu.CompilerParams(vmem_limit_bytes=VMEM_LIMIT),
        cost_estimate=pl.CostEstimate(
            flops=len(entries) * 6 * heads * HD * rows * keys,
            transcendentals=0,
            bytes_accessed=len(entries) * 4 * heads * rows * keys,
        ),
    )(*operands)


def attend_kernel(acc, mine, out):
    for side in range(2):
        inverse = 1.0 / mine[0, 0, 3 * side + 1 : 3 * side + 2]
        out[side * HD : (side + 1) * HD] = (acc[0, side] * inverse).astype(out.dtype)


def acc_rows(member, which, rows):
    return pl.BlockSpec((1, 2, HD, rows), lambda p: (member, p, which, 0))


def attend_terms(member, acc, mine):
    _, heads, _, rows = acc.shape
    return pl.pallas_call(
        attend_kernel,
        grid=(heads // 2,),
        in_specs=[acc_rows(member, 0, rows), member_rows(member, rows)],
        out_specs=pl.BlockSpec((2 * HD, rows), lambda p: (p, 0)),
        out_shape=jax.ShapeDtypeStruct((heads * HD, rows), jnp.bfloat16),
        name="attend_terms",
        compiler_params=pltpu.CompilerParams(vmem_limit_bytes=VMEM_LIMIT),
        cost_estimate=pl.CostEstimate(
            flops=heads * HD * rows, transcendentals=0, bytes_accessed=6 * heads * HD * rows
        ),
    )(acc, mine)


def query_kernel(own, *refs):
    if own:
        first, second, mine, other, upper, came, out_o, out_q = refs
    else:
        first, second, mine, other, out_q = refs
    scale = 1.0 / math.sqrt(HD)
    outs = []
    grads = []
    for side in range(2):
        top, inverse, mean, share = joined(mine.at[0, 0], other.at[0, 0], side)
        factor = jnp.exp2(mine[0, 0, 3 * side : 3 * side + 1] - top) * inverse
        grads.append((second[0, side] - first[0, side] * mean) * (factor * scale))
        if own:
            theirs = came[side * HD : (side + 1) * HD].astype(jnp.float32) * share
            outs.append(upper[0, side] * factor + theirs)
    out_q[...] = jnp.concatenate(grads, axis=0).T.astype(out_q.dtype)
    if own:
        out_o[...] = jnp.concatenate(outs, axis=0).T.astype(out_o.dtype)


def query_terms(member, acc, mine, theirs, came):
    _, heads, _, rows = acc.shape
    own = came is not None
    in_specs = [acc_rows(member, 1, rows), acc_rows(member, 2, rows)]
    in_specs += [member_rows(member, rows), member_rows(1 - member, rows)]
    operands = [acc, acc, mine, theirs]
    shapes = [jax.ShapeDtypeStruct((rows, heads * HD), jnp.float32 if own else jnp.bfloat16)]
    if own:
        in_specs += [acc_rows(member, 0, rows), pl.BlockSpec((2 * HD, rows), lambda p: (p, 0))]
        operands += [acc, came]
        shapes = [jax.ShapeDtypeStruct((rows, heads * HD), jnp.bfloat16)] + shapes
    return pl.pallas_call(
        lambda *refs: query_kernel(own, *refs),
        grid=(heads // 2,),
        in_specs=in_specs,
        out_specs=[column_spec(rows, 0)] * len(shapes),
        out_shape=shapes,
        name="query_own" if own else "query_send",
        compiler_params=pltpu.CompilerParams(vmem_limit_bytes=VMEM_LIMIT),
        cost_estimate=pl.CostEstimate(
            flops=8 * heads * HD * rows, transcendentals=0, bytes_accessed=16 * heads * HD * rows
        ),
    )(*operands)


def final_kernel(query_count, *refs):
    ins, (out_q, out_k, out_v) = refs[:-3], refs[-3:]

    def summed(parts):
        total = parts[0][...].astype(jnp.float32)
        for part in parts[1:]:
            total = total + part[...].astype(jnp.float32)
        return total

    out_q[...] = summed(ins[:query_count]).astype(jnp.bfloat16)
    keys = summed(ins[query_count:])
    features = out_k.shape[1]
    out_k[...] = keys[:, :features].astype(jnp.bfloat16)
    out_v[...] = keys[:, features:].astype(jnp.bfloat16)


def final_sums(query_parts, key_parts):
    rows, features = query_parts[0].shape
    tile = rows // 4
    narrow = pl.BlockSpec((tile, features), lambda p: (p, 0))
    wide = pl.BlockSpec((tile, 2 * features), lambda p: (p, 0))
    return pl.pallas_call(
        lambda *refs: final_kernel(len(query_parts), *refs),
        grid=(rows // tile,),
        in_specs=[narrow] * len(query_parts) + [wide] * len(key_parts),
        out_specs=[narrow] * 3,
        out_shape=[jax.ShapeDtypeStruct((rows, features), jnp.bfloat16)] * 3,
        name="final_sums",
    )(*query_parts, *key_parts)


def swapped(x, offset):
    devices = lax.axis_size("seq")
    return lax.ppermute(x, "seq", [(i, i ^ offset) for i in range(devices)])


def pack_kernel(k_ref, v_ref, q_ref, do_ref, kv_ref, qd_ref):
    features = k_ref.shape[1]
    qd_ref[:, :features] = q_ref[...]
    qd_ref[:, features:] = do_ref[...]
    kv_ref[:, :features] = k_ref[...]
    kv_ref[:, features:] = v_ref[...]


def packed(key_states, value_states, queries, grad_output):
    rows, features = queries.shape
    both = jax.ShapeDtypeStruct((rows, 2 * features), queries.dtype)
    whole = pl.BlockSpec(memory_space=pltpu.VMEM)
    return pl.pallas_call(
        pack_kernel,
        in_specs=[whole] * 4,
        out_specs=[whole] * 2,
        out_shape=[both, both],
        name="pack",
    )(key_states, value_states, queries, grad_output)


def after(x, earlier):
    return lax.optimization_barrier((x, earlier))[0]


def dense_local(queries, key_states, value_states, grad_output, partners, global_blocks):
    devices = lax.axis_size("seq")
    far = devices // 2
    tables = (partners, global_blocks)
    key_value, query_grad = packed(key_states, value_states, queries, grad_output)
    offsets = list(range(far))
    neighbours = [o for o in offsets if o and o & (o - 1) == 0]
    relayed = [o for o in offsets if o and o not in neighbours]
    query_blocks = [(0, query_grad), (far, swapped(query_grad, far))]
    blocks = {0: key_value}
    for o in neighbours:
        blocks[o] = swapped(key_value, o)
    saved = {}
    last = [None]

    def run(pairs, members, running):
        used = sorted({k for _, k in pairs})
        key_blocks = [(k, blocks[k]) for k in used]
        if last[0] is not None:
            key_blocks = [(k, after(x, last[0])) for k, x in key_blocks]
        plan = tuple((q, used.index(k)) for q, k in pairs)
        e, u, acc, state, stat = pair_terms(
            tables, plan, query_blocks[:members], key_blocks, running
        )
        for at, (q, k) in enumerate(pairs):
            base = at * (stat.shape[0] // len(pairs))
            saved[(q, k)] = (e, u, query_blocks[q][1], stat, base)
        last[0] = stat
        return (acc, state)

    running = run([(0, 0)], 1, None)
    for o in neighbours[:-1]:
        running = run([(0, o)], 1, running)
    for o in relayed:
        lowest = o & -o
        blocks[o] = swapped(after(blocks[o - lowest], last[0]), lowest)
    rest = [(0, neighbours[-1])] + [(1, o) for o in [0] + neighbours]
    running = run(rest, 2, running)
    acc, mine = run([(q, o) for o in relayed for q in (1, 0)], 2, running)
    theirs = swapped(mine, far)
    upper = attend_terms(1, acc, mine)
    came_upper = swapped(upper, far)
    key_parts = []
    theirs = after(theirs, upper)
    for k in offsets[:0:-1]:
        entries = [saved[(q, k)] for q in range(2)]
        terms = key_terms(entries, mine, after(theirs, last[0]), jnp.bfloat16)
        key_parts.append(swapped(terms, k))
        last[0] = terms
        if len(key_parts) == 1:
            sent = query_terms(1, acc, mine, after(theirs, terms), None)[0]
            came = swapped(sent, far)
            last[0] = sent
    own_entries = [saved[(q, 0)] for q in range(2)]
    own_keys = key_terms(own_entries, mine, after(theirs, last[0]), jnp.float32)
    came_upper = after(came_upper, own_keys)
    attended, own_queries = query_terms(0, acc, mine, theirs, came_upper)
    came = after(came, own_queries)
    return (attended,) + tuple(final_sums([own_queries, came], [own_keys] + key_parts))


def paired(devices):
    return 4 <= devices <= LISTED and devices & (devices - 1) == 0


def local(*operands):
    if paired(lax.axis_size("seq")):
        return dense_local(*operands)
    return routed_local(*operands)


def solution(mesh):
    in_specs = (
        P(("batch", "seq"), None),
        P(("batch", "seq"), None),
        P(("batch", "seq"), None),
        P(("batch", "seq"), None),
        P("batch", None),
        P("batch"),
    )
    out_specs = (
        P(("batch", "seq"), None),
        P(("batch", "seq"), None),
        P(("batch", "seq"), None),
        P(("batch", "seq"), None),
    )
    step = jax.shard_map(
        local, mesh=mesh, in_specs=in_specs, out_specs=out_specs, check_vma=False
    )
    devices = mesh.shape["seq"]
    if paired(devices):
        return step
    return step
```

```python
import math

import jax
import jax.numpy as jnp
from jax import lax
from jax.experimental import pallas as pl
from jax.experimental.pallas import tpu as pltpu
from jax.sharding import PartitionSpec as P

HEADS = 6
HD = 64


def extended(x, sides, width):
    for axis, dim in sides:
        devices, length = (lax.axis_size(axis), x.shape[dim])
        up = [(i, (i + 1) % devices) for i in range(devices)]
        down = [(j, i) for i, j in up]
        last = lax.slice_in_dim(x, length - width, length, axis=dim)
        first = lax.slice_in_dim(x, 0, width, axis=dim)
        before = lax.ppermute(last, axis, up)
        after = lax.ppermute(first, axis, down)
        x = jnp.concatenate([before, x, after], axis=dim)
    return x


def from_behind(x, axis, by):
    devices = lax.axis_size(axis)
    return lax.ppermute(x, axis, [(i, (i + by) % devices) for i in range(devices)])


def head_split(matrix):
    return matrix.reshape(matrix.shape[0], HEADS, HD).transpose(1, 0, 2)


def head_join(stacked):
    return stacked.transpose(1, 0, 2).reshape(stacked.shape[1], HEADS * HD)


def attend(queries, key_rows, grad_output):
    features = queries.shape[1]
    scale = 1.0 / math.sqrt(HD)
    contract_last = (((1,), (1,)), ((), ()))
    contract_first = (((0,), (0,)), ((), ()))

    def per_head(head_items):
        query_head, key_head, value_head, grad_head = head_items
        scores = (
            lax.dot_general(query_head, key_head, contract_last, preferred_element_type=jnp.float32)
            * scale
        )
        row_peak = jnp.max(scores, axis=-1, keepdims=True)
        exponent = jnp.exp(scores - row_peak)
        weights = exponent / jnp.sum(exponent, axis=-1, keepdims=True)
        weights_low = weights.astype(jnp.bfloat16)
        output_head = jnp.dot(weights_low, value_head, preferred_element_type=jnp.float32).astype(
            jnp.bfloat16
        )
        grad_weights = lax.dot_general(
            grad_head, value_head, contract_last, preferred_element_type=jnp.float32
        )
        row_dots = jnp.sum(weights * grad_weights, axis=-1, keepdims=True)
        grad_scores = (weights * (grad_weights - row_dots) * scale).astype(jnp.bfloat16)
        grad_query = jnp.dot(grad_scores, key_head, preferred_element_type=jnp.float32).astype(
            jnp.bfloat16
        )
        grad_key = lax.dot_general(
            grad_scores, query_head, contract_first, preferred_element_type=jnp.float32
        )
        grad_value = lax.dot_general(
            weights_low, grad_head, contract_first, preferred_element_type=jnp.float32
        )
        return (output_head, grad_query, grad_key, grad_value)

    outputs, grad_query, grad_key, grad_value = lax.map(
        per_head,
        (
            head_split(queries),
            head_split(key_rows[:, :features]),
            head_split(key_rows[:, features:]),
            head_split(grad_output),
        ),
    )
    grad_pair = jnp.concatenate([head_join(grad_key), head_join(grad_value)], axis=1)
    return (head_join(outputs), head_join(grad_query), grad_pair)


def route_forward(key_value, route_table, devices):
    block_rows, columns = key_value.shape
    pieces = key_value.reshape(devices, block_rows // devices, columns)
    spread = lax.all_to_all(pieces, "seq", split_axis=0, concat_axis=0, tiled=True)
    picked = jnp.take(spread, route_table, axis=0)
    arrived = lax.all_to_all(picked, "seq", split_axis=1, concat_axis=1, tiled=True)
    return arrived.reshape(route_table.shape[0], block_rows, columns)


def route_back(grad_terms, route_table, devices):
    routes, block_rows, columns = grad_terms.shape
    piece_rows = block_rows // devices
    pieces = grad_terms.reshape(routes, devices, piece_rows, columns)
    coming = lax.all_to_all(pieces, "seq", split_axis=1, concat_axis=1, tiled=True)
    block_ids = jnp.arange(devices, dtype=jnp.int32)
    one_hot = (route_table[:, :, None] == block_ids[None, None, :]).astype(jnp.float32)
    summed = jnp.einsum(
        "rds,rdx->sx",
        one_hot,
        coming.reshape(routes, devices, piece_rows * columns),
        precision=lax.Precision.HIGHEST,
    )
    returned = lax.all_to_all(
        summed.reshape(devices, piece_rows, columns), "seq", split_axis=0, concat_axis=0, tiled=True
    )
    return returned.reshape(block_rows, columns)


def routed_local(queries, key_states, value_states, grad_output, partners, global_blocks):
    devices = lax.axis_size("seq")
    block_rows = queries.shape[0]
    features = queries.shape[1]
    key_value = jnp.concatenate([key_states, value_states], axis=1)
    table_rows = []
    table_rows = table_rows + [partners[0], partners[1], partners[2]]
    table_rows = table_rows + [
        jnp.full((devices,), global_blocks[0], jnp.int32),
        jnp.full((devices,), global_blocks[1], jnp.int32),
    ]
    route_table = jnp.stack(table_rows)
    fetched = route_forward(key_value, route_table, devices)
    padded = extended(key_value, (("seq", 0),), block_rows)
    left_block = padded[:block_rows]
    right_block = padded[2 * block_rows :]
    offset = 0
    random_blocks = [fetched[offset], fetched[offset + 1], fetched[offset + 2]]
    global_rows = [fetched[offset + 3], fetched[offset + 4]]
    key_rows = jnp.concatenate(
        [key_value, left_block, right_block] + random_blocks + global_rows, axis=0
    )
    attended, grad_queries, grad_pair = attend(queries, key_rows, grad_output)
    grad_parts = grad_pair.reshape(8, block_rows, 2 * features)
    grad_total = grad_parts[0]
    returning = []
    grad_total = grad_total + from_behind(grad_parts[1], "seq", -1)
    grad_total = grad_total + from_behind(grad_parts[2], "seq", 1)
    returning = returning + [grad_parts[3], grad_parts[4], grad_parts[5]]
    returning = returning + [grad_parts[6], grad_parts[7]]
    grad_total = grad_total + route_back(jnp.stack(returning), route_table, devices)
    return (
        attended,
        grad_queries,
        grad_total[:, :features].astype(jnp.bfloat16),
        grad_total[:, features:].astype(jnp.bfloat16),
    )


ORDER = [
    "p0",
    "c0",
    "p1",
    "e0",
    "c1",
    "f0",
    "s0",
    "p2",
    "e1",
    "c2",
    "s1",
    "p3",
    "e2",
    "c3",
    "f2",
    "s2",
    "f1",
    "e3",
    "f3",
    "s3",
]
LISTED = 8
TO_LOG2 = 1.0 / (math.log(2.0) * math.sqrt(HD))
VMEM_LIMIT = 40 * 1024 * 1024
PAIR_LIMIT = 40 * 1024 * 1024


def matmul(a, b, contract_a, contract_b):
    return lax.dot_general(
        a, b, (((contract_a,), (contract_b,)), ((), ())), preferred_element_type=jnp.float32
    )


def placed(rows, side):
    blank = jnp.zeros_like(rows)
    return jnp.concatenate([rows, blank] if side == 0 else [blank, rows], axis=0)


def listed_times(partners_ref, globals_ref, query_block, key_block, devices):
    count = jnp.int32(0)
    entries = [query_block, lax.rem(query_block + devices - 1, devices)]
    entries += [lax.rem(query_block + 1, devices)]
    entries += [partners_ref[r, query_block] for r in range(partners_ref.shape[0])]
    entries += [globals_ref[g] for g in range(globals_ref.shape[0])]
    for entry in entries:
        count = count + jnp.where(entry == key_block, 1, 0)
    return count


def chosen(index, values):
    result = values[0]
    for at in range(1, len(values)):
        result = jnp.where(index == at, values[at], result)
    return result


def pairs_kernel(plan, partners_ref, globals_ref, *refs):
    pairs, query_moves, key_moves, carried = plan
    queries, keys = len(query_moves), len(key_moves)
    query_refs = refs[: 2 * queries]
    key_refs = refs[2 * queries : 2 * (queries + keys)]
    refs = refs[2 * (queries + keys) :]
    if carried:
        acc_in, run_in = refs[:2]
        refs = refs[2:]
    e_ref, u_ref, acc_ref, run_ref, pair_ref = refs[:5]
    q_now, do_now, k_now, v_now, low_kept, both_kept, peak_kept, v_kept, kt_kept, dt_kept = refs[5:]
    step = pl.program_id(0)
    total_steps = pl.num_programs(0) - 1
    per_pair = total_steps // len(pairs)
    now = jnp.minimum(step, total_steps - 1)
    then = jnp.maximum(step - 1, 0)
    slot, old_slot = lax.rem(step, 2), lax.rem(step + 1, 2)
    pair_now, pair_then = now // per_pair, then // per_pair
    group = lax.rem(then, per_pair)
    for at in range(queries):

        @pl.when(chosen(pair_now, [q for q, _ in pairs]) == at)
        def _():
            q_now[...] = query_refs[2 * at][...]
            do_now[...] = query_refs[2 * at + 1][...]

    for at in range(keys):

        @pl.when(chosen(pair_now, [k for _, k in pairs]) == at)
        def _():
            k_now[...] = key_refs[2 * at][...]
            v_now[...] = key_refs[2 * at + 1][...]

    chunk = q_now.shape[0] // 2
    devices = lax.axis_size("seq")
    me = lax.axis_index("seq")
    count = listed_times(
        partners_ref,
        globals_ref,
        me ^ chosen(pair_then, [query_moves[q] for q, _ in pairs]),
        me ^ chosen(pair_then, [key_moves[k] for _, k in pairs]),
        devices,
    ).astype(jnp.float32)
    bias = jnp.log2(jnp.full((1, chunk), jnp.maximum(count, 1.0), jnp.float32))
    bias = jnp.where(count > 0.0, bias, -1e30)
    member = chosen(pair_then, [q for q, _ in pairs])
    first_head = 2 * group

    key_rows = k_now[...]
    values = v_now[...]
    keys_twice = jnp.concatenate([key_rows, key_rows], axis=1)
    q_t = q_now[...].T.astype(jnp.float32) * TO_LOG2
    q_high = q_t.astype(jnp.bfloat16)
    q_low = (q_t - q_high.astype(jnp.float32)).astype(jnp.bfloat16)
    k_t = key_rows.T
    v_t = values.T
    v_kept[slot] = values
    kt_kept[slot] = k_t
    dt_kept[slot] = do_now[...].T
    ones = jnp.ones((16, key_rows.shape[0]), jnp.bfloat16)
    units = [(side, at) for side in range(2) for at in range(2)]
    halves = [slice(0, HD), slice(HD, 2 * HD)]
    lanes = [slice(at * chunk, (at + 1) * chunk) for at in range(2)]
    scores = {}
    lows = {}
    centred = {}

    def products(n):
        side, at = units[n]
        both_q = [placed(x[halves[side], lanes[at]], side) for x in (q_high, q_low)]
        scores[n] = matmul(keys_twice, jnp.concatenate(both_q, axis=0), 1, 0)

    def exponents(n):
        side, at = units[n]
        peak = jnp.max(scores[n], axis=0, keepdims=True)
        low = jnp.exp2(scores.pop(n) - peak).astype(jnp.bfloat16)
        e_ref[0, side, :, lanes[at]] = low
        low_kept[slot, side, :, lanes[at]] = low
        peak_kept[slot, side : side + 1, lanes[at]] = peak
        lows[n] = low

    def sums(n):
        side, at = units[n]
        left = jnp.concatenate([v_t[halves[side]], k_t[halves[side]], ones], axis=0)
        both_kept[slot, side, :, lanes[at]] = matmul(left, lows.pop(n), 1, 0)

    def centre(n):
        side, at = units[n]
        cols = lanes[at]
        do_t = dt_kept[old_slot, halves[side], cols]
        upper = both_kept[old_slot, side, :HD, cols]
        total = both_kept[old_slot, side, 2 * HD : 2 * HD + 1, cols]
        dots = jnp.sum(upper * do_t.astype(jnp.float32), axis=0, keepdims=True)
        mean = dots / total
        grad = matmul(v_kept[old_slot], placed(do_t, side), 1, 0)
        shifted = low_kept[old_slot, side, :, cols] * (grad - mean).astype(jnp.bfloat16)
        u_ref[0, side, :, cols] = shifted
        centred[n] = (shifted, total, dots, mean)

    def finish(n):
        side, at = units[n]
        cols = lanes[at]
        shifted, total, dots, mean = centred.pop(n)
        both = both_kept[old_slot, side, : 2 * HD, cols]
        moved = matmul(kt_kept[old_slot, halves[side]], shifted, 1, 0) + mean * both[HD:]
        peak = peak_kept[old_slot, side : side + 1, cols] + bias
        head = first_head + side
        row = 3 * side
        old = run_ref[member, group, row : row + 1, cols]
        top = jnp.maximum(old, peak)
        keep = jnp.exp2(old - top)
        take = jnp.exp2(peak - top)
        acc_ref[member, head, : 2 * HD, cols] = (
            acc_ref[member, head, : 2 * HD, cols] * keep + both * take
        )
        acc_ref[member, head, 2 * HD :, cols] = (
            acc_ref[member, head, 2 * HD :, cols] * keep + moved * take
        )
        total = run_ref[member, group, row + 1 : row + 2, cols] * keep + total * take
        dots = run_ref[member, group, row + 2 : row + 3, cols] * keep + dots * take
        for at_row, value in enumerate((top, total, dots)):
            run_ref[member, group, row + at_row : row + at_row + 1, cols] = value
        for at_row, value in enumerate((peak, mean)):
            pair_ref[0, row + at_row : row + at_row + 1, cols] = value

    stages = dict(p=products, e=exponents, s=sums, c=centre, f=finish)
    for name in ORDER:
        stages[name[0]](int(name[1:]))

    @pl.when(step == 0)
    def _():
        acc_ref[...] = jnp.zeros_like(acc_ref)
        run_ref[...] = jnp.zeros_like(run_ref)
        for member_at in range(acc_ref.shape[0]):
            if member_at < carried:
                acc_ref[member_at] = acc_in[member_at]
                run_ref[member_at] = run_in[member_at]
            else:
                for row in (0, 3):
                    shape = (run_ref.shape[1], 1, run_ref.shape[3])
                    run_ref[member_at, :, row : row + 1] = jnp.full(shape, -1e30, jnp.float32)


def head_pairs(features):
    return features // (2 * HD)


def column_spec(rows, offset):
    return pl.BlockSpec((rows, 2 * HD), lambda p: (0, p + offset))


def step_spec(offset, steps, used, last, *block):
    def index(p):
        now = jnp.minimum(p, last)
        live = sum(jnp.where(now // steps == at, 1, 0) for at in used)
        return (0, lax.rem(now, steps) * live + offset)

    return pl.BlockSpec(block, index)


def pair_terms(tables, pairs, query_blocks, key_blocks, running):
    query_moves, query_arrays = zip(*query_blocks)
    key_moves, key_arrays = zip(*key_blocks)
    rows, columns = query_arrays[0].shape
    keys = key_arrays[0].shape[0]
    features = columns // 2
    steps = head_pairs(features)
    heads = 2 * steps
    total = len(pairs) * steps
    members = len(query_arrays)
    state = [] if running is None else list(running)
    carried = state[0].shape[0] if state else 0
    plan = (pairs, query_moves, key_moves, carried)
    acc = jax.ShapeDtypeStruct((members, heads, 3 * HD, rows), jnp.float32)
    run = jax.ShapeDtypeStruct((members, steps, 8, rows), jnp.float32)
    stat = jax.ShapeDtypeStruct((total, 8, rows), jnp.float32)
    big = jax.ShapeDtypeStruct((total, 2, keys, rows), jnp.bfloat16)
    operands = []
    in_specs = [pl.BlockSpec(memory_space=pltpu.SMEM)] * 2
    for kind, arrays in ((0, query_arrays), (1, key_arrays)):
        for which, array in enumerate(arrays):
            used = [at for at, pair in enumerate(pairs) if pair[kind] == which]
            length = array.shape[0]
            in_specs.append(step_spec(0, steps, used, total - 1, length, 2 * HD))
            in_specs.append(step_spec(steps, steps, used, total - 1, length, 2 * HD))
            operands += [array, array]
    whole = pl.BlockSpec(memory_space=pltpu.VMEM)
    in_specs += [whole] * len(state)
    now = lambda p: (jnp.minimum(p, total - 1), 0, 0, 0)
    then = lambda p: (jnp.maximum(p - 1, 0), 0, 0, 0)
    block = (1, 2, keys, rows)
    tile = pltpu.VMEM((rows, 2 * HD), jnp.bfloat16)
    return pl.pallas_call(
        lambda *refs: pairs_kernel(plan, *refs),
        grid=(total + 1,),
        in_specs=in_specs,
        out_specs=[
            pl.BlockSpec(block, now),
            pl.BlockSpec(block, then),
            whole,
            whole,
            pl.BlockSpec((1, 8, rows), lambda p: then(p)[:3]),
        ],
        out_shape=[big, big, acc, run, stat],
        scratch_shapes=[
            tile,
            tile,
            pltpu.VMEM((keys, 2 * HD), jnp.bfloat16),
            pltpu.VMEM((keys, 2 * HD), jnp.bfloat16),
            pltpu.VMEM((2, 2, keys, rows), jnp.bfloat16),
            pltpu.VMEM((2, 2, 2 * HD + 16, rows), jnp.float32),
            pltpu.VMEM((2, 8, rows), jnp.float32),
            pltpu.VMEM((2, keys, 2 * HD), jnp.bfloat16),
            pltpu.VMEM((2, 2 * HD, keys), jnp.bfloat16),
            pltpu.VMEM((2, 2 * HD, rows), jnp.bfloat16),
        ],
        compiler_params=pltpu.CompilerParams(vmem_limit_bytes=PAIR_LIMIT),
        cost_estimate=pl.CostEstimate(
            flops=len(pairs) * 8 * heads * HD * rows * keys,
            transcendentals=len(pairs) * heads * rows * keys,
            bytes_accessed=len(pairs) * 4 * heads * rows * keys,
        ),
    )(*tables, *operands, *state)


def joined(mine, other, side):
    at = 3 * side
    top = jnp.maximum(mine[at : at + 1], other[at : at + 1])
    here = jnp.exp2(mine[at : at + 1] - top)
    there = jnp.exp2(other[at : at + 1] - top)
    inverse = 1.0 / (mine[at + 1 : at + 2] * here + other[at + 1 : at + 2] * there)
    mean = (mine[at + 2 : at + 3] * here + other[at + 2 : at + 3] * there) * inverse
    share = other[at + 1 : at + 2] * there * inverse
    return top, inverse, mean, share


def key_kernel(*refs):
    out = refs[-1]
    features = out.shape[1] // 2
    scale = 1.0 / math.sqrt(HD)
    k_total = None
    v_total = None
    for at in range(0, len(refs) - 1, 7):
        e_ref, u_ref, q_ref, do_ref, pair_ref, mine, other = refs[at : at + 7]
        q_t = q_ref[...].T.astype(jnp.float32)
        do_t = do_ref[...].T.astype(jnp.float32)
        for side in range(2):
            rows = slice(side * HD, (side + 1) * HD)
            top, inverse, mean, _ = joined(mine.at[0, 0], other.at[0, 0], side)
            factor = jnp.exp2(pair_ref[0, 3 * side : 3 * side + 1] - top) * inverse
            shift = pair_ref[0, 3 * side + 1 : 3 * side + 2] - mean
            scaled_q = q_t[rows] * (factor * scale)
            for_e = jnp.concatenate(
                [
                    placed((scaled_q * shift).astype(jnp.bfloat16), side),
                    placed((do_t[rows] * factor).astype(jnp.bfloat16), side),
                ],
                axis=0,
            )
            from_e = matmul(e_ref[0, side], for_e, 1, 1)
            from_u = matmul(u_ref[0, side], placed(scaled_q.astype(jnp.bfloat16), side), 1, 1)
            k_part = from_e[:, : 2 * HD] + from_u
            v_part = from_e[:, 2 * HD :]
            k_total = k_part if k_total is None else k_total + k_part
            v_total = v_part if v_total is None else v_total + v_part
    at = pl.program_id(0) * (2 * HD)
    out[:, pl.ds(pl.multiple_of(at, 2 * HD), 2 * HD)] = k_total.astype(out.dtype)
    at = at + features
    out[:, pl.ds(pl.multiple_of(at, 2 * HD), 2 * HD)] = v_total.astype(out.dtype)


def member_rows(member, rows):
    return pl.BlockSpec((1, 1, 8, rows), lambda p: (member, p, 0, 0))


def key_terms(entries, mine, theirs, dtype):
    operands = []
    in_specs = []
    for member, (e, u, query_grad, stat, base) in enumerate(entries):
        _, _, keys, rows = e.shape
        steps = head_pairs(query_grad.shape[1] // 2)
        block = pl.BlockSpec((1, 2, keys, rows), lambda p, base=base: (p + base, 0, 0, 0))
        operands += [e, u, query_grad, query_grad, stat, mine, theirs]
        in_specs += [
            block,
            block,
            column_spec(rows, 0),
            column_spec(rows, steps),
            pl.BlockSpec((1, 8, rows), lambda p, base=base: (p + base, 0, 0)),
            member_rows(member, rows),
            member_rows(1 - member, rows),
        ]
    heads = 2 * steps
    return pl.pallas_call(
        key_kernel,
        grid=(steps,),
        in_specs=in_specs,
        out_specs=pl.BlockSpec(memory_space=pltpu.VMEM),
        out_shape=jax.ShapeDtypeStruct((keys, 2 * heads * HD), dtype),
        name="key_terms",
        compiler_params=pltpu.CompilerParams(vmem_limit_bytes=VMEM_LIMIT),
        cost_estimate=pl.CostEstimate(
            flops=len(entries) * 6 * heads * HD * rows * keys,
            transcendentals=0,
            bytes_accessed=len(entries) * 4 * heads * rows * keys,
        ),
    )(*operands)


def attend_kernel(acc, mine, out):
    for side in range(2):
        inverse = 1.0 / mine[0, 0, 3 * side + 1 : 3 * side + 2]
        out[side * HD : (side + 1) * HD] = (acc[0, side] * inverse).astype(out.dtype)


def acc_rows(member, which, rows):
    return pl.BlockSpec((1, 2, HD, rows), lambda p: (member, p, which, 0))


def attend_terms(member, acc, mine):
    _, heads, _, rows = acc.shape
    return pl.pallas_call(
        attend_kernel,
        grid=(heads // 2,),
        in_specs=[acc_rows(member, 0, rows), member_rows(member, rows)],
        out_specs=pl.BlockSpec((2 * HD, rows), lambda p: (p, 0)),
        out_shape=jax.ShapeDtypeStruct((heads * HD, rows), jnp.bfloat16),
        name="attend_terms",
        compiler_params=pltpu.CompilerParams(vmem_limit_bytes=VMEM_LIMIT),
        cost_estimate=pl.CostEstimate(
            flops=heads * HD * rows, transcendentals=0, bytes_accessed=6 * heads * HD * rows
        ),
    )(acc, mine)


def query_kernel(own, *refs):
    if own:
        first, second, mine, other, upper, came, out_o, out_q = refs
    else:
        first, second, mine, other, out_q = refs
    scale = 1.0 / math.sqrt(HD)
    outs = []
    grads = []
    for side in range(2):
        top, inverse, mean, share = joined(mine.at[0, 0], other.at[0, 0], side)
        factor = jnp.exp2(mine[0, 0, 3 * side : 3 * side + 1] - top) * inverse
        grads.append((second[0, side] - first[0, side] * mean) * (factor * scale))
        if own:
            theirs = came[side * HD : (side + 1) * HD].astype(jnp.float32) * share
            outs.append(upper[0, side] * factor + theirs)
    out_q[...] = jnp.concatenate(grads, axis=0).T.astype(out_q.dtype)
    if own:
        out_o[...] = jnp.concatenate(outs, axis=0).T.astype(out_o.dtype)


def query_terms(member, acc, mine, theirs, came):
    _, heads, _, rows = acc.shape
    own = came is not None
    in_specs = [acc_rows(member, 1, rows), acc_rows(member, 2, rows)]
    in_specs += [member_rows(member, rows), member_rows(1 - member, rows)]
    operands = [acc, acc, mine, theirs]
    shapes = [jax.ShapeDtypeStruct((rows, heads * HD), jnp.float32 if own else jnp.bfloat16)]
    if own:
        in_specs += [acc_rows(member, 0, rows), pl.BlockSpec((2 * HD, rows), lambda p: (p, 0))]
        operands += [acc, came]
        shapes = [jax.ShapeDtypeStruct((rows, heads * HD), jnp.bfloat16)] + shapes
    return pl.pallas_call(
        lambda *refs: query_kernel(own, *refs),
        grid=(heads // 2,),
        in_specs=in_specs,
        out_specs=[column_spec(rows, 0)] * len(shapes),
        out_shape=shapes,
        name="query_own" if own else "query_send",
        compiler_params=pltpu.CompilerParams(vmem_limit_bytes=VMEM_LIMIT),
        cost_estimate=pl.CostEstimate(
            flops=8 * heads * HD * rows, transcendentals=0, bytes_accessed=16 * heads * HD * rows
        ),
    )(*operands)


def final_kernel(query_count, *refs):
    ins, (out_q, out_k, out_v) = refs[:-3], refs[-3:]

    def summed(parts):
        total = parts[0][...].astype(jnp.float32)
        for part in parts[1:]:
            total = total + part[...].astype(jnp.float32)
        return total

    out_q[...] = summed(ins[:query_count]).astype(jnp.bfloat16)
    keys = summed(ins[query_count:])
    features = out_k.shape[1]
    out_k[...] = keys[:, :features].astype(jnp.bfloat16)
    out_v[...] = keys[:, features:].astype(jnp.bfloat16)


def final_sums(query_parts, key_parts):
    rows, features = query_parts[0].shape
    tile = rows // 4
    narrow = pl.BlockSpec((tile, features), lambda p: (p, 0))
    wide = pl.BlockSpec((tile, 2 * features), lambda p: (p, 0))
    return pl.pallas_call(
        lambda *refs: final_kernel(len(query_parts), *refs),
        grid=(rows // tile,),
        in_specs=[narrow] * len(query_parts) + [wide] * len(key_parts),
        out_specs=[narrow] * 3,
        out_shape=[jax.ShapeDtypeStruct((rows, features), jnp.bfloat16)] * 3,
        name="final_sums",
    )(*query_parts, *key_parts)


def swapped(x, offset):
    devices = lax.axis_size("seq")
    return lax.ppermute(x, "seq", [(i, i ^ offset) for i in range(devices)])


def pack_kernel(k_ref, v_ref, q_ref, do_ref, kv_ref, qd_ref):
    features = k_ref.shape[1]
    qd_ref[:, :features] = q_ref[...]
    qd_ref[:, features:] = do_ref[...]
    kv_ref[:, :features] = k_ref[...]
    kv_ref[:, features:] = v_ref[...]


def packed(key_states, value_states, queries, grad_output):
    rows, features = queries.shape
    both = jax.ShapeDtypeStruct((rows, 2 * features), queries.dtype)
    whole = pl.BlockSpec(memory_space=pltpu.VMEM)
    return pl.pallas_call(
        pack_kernel,
        in_specs=[whole] * 4,
        out_specs=[whole] * 2,
        out_shape=[both, both],
        name="pack",
    )(key_states, value_states, queries, grad_output)


def after(x, earlier):
    return lax.optimization_barrier((x, earlier))[0]


def dense_local(queries, key_states, value_states, grad_output, partners, global_blocks):
    devices = lax.axis_size("seq")
    far = devices // 2
    tables = (partners, global_blocks)
    key_value, query_grad = packed(key_states, value_states, queries, grad_output)
    offsets = list(range(far))
    neighbours = [o for o in offsets if o and o & (o - 1) == 0]
    relayed = [o for o in offsets if o and o not in neighbours]
    query_blocks = [(0, query_grad), (far, swapped(query_grad, far))]
    blocks = {0: key_value}
    for o in neighbours:
        blocks[o] = swapped(key_value, o)
    saved = {}
    last = [None]

    def run(pairs, members, running):
        used = sorted({k for _, k in pairs})
        key_blocks = [(k, blocks[k]) for k in used]
        if last[0] is not None:
            key_blocks = [(k, after(x, last[0])) for k, x in key_blocks]
        plan = tuple((q, used.index(k)) for q, k in pairs)
        e, u, acc, state, stat = pair_terms(
            tables, plan, query_blocks[:members], key_blocks, running
        )
        for at, (q, k) in enumerate(pairs):
            base = at * (stat.shape[0] // len(pairs))
            saved[(q, k)] = (e, u, query_blocks[q][1], stat, base)
        last[0] = stat
        return (acc, state)

    running = run([(0, 0)], 1, None)
    for o in neighbours[:-1]:
        running = run([(0, o)], 1, running)
    for o in relayed:
        lowest = o & -o
        blocks[o] = swapped(after(blocks[o - lowest], last[0]), lowest)
    rest = [(0, neighbours[-1])] + [(1, o) for o in [0] + neighbours]
    running = run(rest, 2, running)
    acc, mine = run([(q, o) for o in relayed for q in (1, 0)], 2, running)
    theirs = swapped(mine, far)
    upper = attend_terms(1, acc, mine)
    came_upper = swapped(after(upper, theirs), far)
    key_parts = []
    for k in offsets[:0:-1]:
        entries = [saved[(q, k)] for q in range(2)]
        terms = key_terms(entries, mine, after(theirs, last[0]), jnp.bfloat16)
        key_parts.append(swapped(terms, k))
        last[0] = terms
        if len(key_parts) == 1:
            sent = query_terms(1, acc, mine, after(theirs, terms), None)[0]
            came = swapped(sent, far)
            last[0] = sent
    own_entries = [saved[(q, 0)] for q in range(2)]
    own_keys = key_terms(own_entries, mine, after(theirs, last[0]), jnp.float32)
    came_upper = after(came_upper, own_keys)
    attended, own_queries = query_terms(0, acc, mine, theirs, came_upper)
    came = after(came, own_queries)
    return (attended,) + tuple(final_sums([own_queries, came], [own_keys] + key_parts))


def paired(devices):
    return 4 <= devices <= LISTED and devices & (devices - 1) == 0


def local(*operands):
    if paired(lax.axis_size("seq")):
        return dense_local(*operands)
    return routed_local(*operands)


def solution(mesh):
    in_specs = (
        P(("batch", "seq"), None),
        P(("batch", "seq"), None),
        P(("batch", "seq"), None),
        P(("batch", "seq"), None),
        P("batch", None),
        P("batch"),
    )
    out_specs = (
        P(("batch", "seq"), None),
        P(("batch", "seq"), None),
        P(("batch", "seq"), None),
        P(("batch", "seq"), None),
    )
    step = jax.shard_map(
        local, mesh=mesh, in_specs=in_specs, out_specs=out_specs, check_vma=False
    )
    devices = mesh.shape["seq"]
    if paired(devices):
        return step
    return step
```

```python
import math

import jax
import jax.numpy as jnp
from jax import lax
from jax.experimental import pallas as pl
from jax.experimental.pallas import tpu as pltpu
from jax.sharding import PartitionSpec as P

HEADS = 6
HD = 64


def extended(x, sides, width):
    for axis, dim in sides:
        devices, length = (lax.axis_size(axis), x.shape[dim])
        up = [(i, (i + 1) % devices) for i in range(devices)]
        down = [(j, i) for i, j in up]
        last = lax.slice_in_dim(x, length - width, length, axis=dim)
        first = lax.slice_in_dim(x, 0, width, axis=dim)
        before = lax.ppermute(last, axis, up)
        after = lax.ppermute(first, axis, down)
        x = jnp.concatenate([before, x, after], axis=dim)
    return x


def from_behind(x, axis, by):
    devices = lax.axis_size(axis)
    return lax.ppermute(x, axis, [(i, (i + by) % devices) for i in range(devices)])


def head_split(matrix):
    return matrix.reshape(matrix.shape[0], HEADS, HD).transpose(1, 0, 2)


def head_join(stacked):
    return stacked.transpose(1, 0, 2).reshape(stacked.shape[1], HEADS * HD)


def attend(queries, key_rows, grad_output):
    features = queries.shape[1]
    scale = 1.0 / math.sqrt(HD)
    contract_last = (((1,), (1,)), ((), ()))
    contract_first = (((0,), (0,)), ((), ()))

    def per_head(head_items):
        query_head, key_head, value_head, grad_head = head_items
        scores = (
            lax.dot_general(query_head, key_head, contract_last, preferred_element_type=jnp.float32)
            * scale
        )
        row_peak = jnp.max(scores, axis=-1, keepdims=True)
        exponent = jnp.exp(scores - row_peak)
        weights = exponent / jnp.sum(exponent, axis=-1, keepdims=True)
        weights_low = weights.astype(jnp.bfloat16)
        output_head = jnp.dot(weights_low, value_head, preferred_element_type=jnp.float32).astype(
            jnp.bfloat16
        )
        grad_weights = lax.dot_general(
            grad_head, value_head, contract_last, preferred_element_type=jnp.float32
        )
        row_dots = jnp.sum(weights * grad_weights, axis=-1, keepdims=True)
        grad_scores = (weights * (grad_weights - row_dots) * scale).astype(jnp.bfloat16)
        grad_query = jnp.dot(grad_scores, key_head, preferred_element_type=jnp.float32).astype(
            jnp.bfloat16
        )
        grad_key = lax.dot_general(
            grad_scores, query_head, contract_first, preferred_element_type=jnp.float32
        )
        grad_value = lax.dot_general(
            weights_low, grad_head, contract_first, preferred_element_type=jnp.float32
        )
        return (output_head, grad_query, grad_key, grad_value)

    outputs, grad_query, grad_key, grad_value = lax.map(
        per_head,
        (
            head_split(queries),
            head_split(key_rows[:, :features]),
            head_split(key_rows[:, features:]),
            head_split(grad_output),
        ),
    )
    grad_pair = jnp.concatenate([head_join(grad_key), head_join(grad_value)], axis=1)
    return (head_join(outputs), head_join(grad_query), grad_pair)


def route_forward(key_value, route_table, devices):
    block_rows, columns = key_value.shape
    pieces = key_value.reshape(devices, block_rows // devices, columns)
    spread = lax.all_to_all(pieces, "seq", split_axis=0, concat_axis=0, tiled=True)
    picked = jnp.take(spread, route_table, axis=0)
    arrived = lax.all_to_all(picked, "seq", split_axis=1, concat_axis=1, tiled=True)
    return arrived.reshape(route_table.shape[0], block_rows, columns)


def route_back(grad_terms, route_table, devices):
    routes, block_rows, columns = grad_terms.shape
    piece_rows = block_rows // devices
    pieces = grad_terms.reshape(routes, devices, piece_rows, columns)
    coming = lax.all_to_all(pieces, "seq", split_axis=1, concat_axis=1, tiled=True)
    block_ids = jnp.arange(devices, dtype=jnp.int32)
    one_hot = (route_table[:, :, None] == block_ids[None, None, :]).astype(jnp.float32)
    summed = jnp.einsum(
        "rds,rdx->sx",
        one_hot,
        coming.reshape(routes, devices, piece_rows * columns),
        precision=lax.Precision.HIGHEST,
    )
    returned = lax.all_to_all(
        summed.reshape(devices, piece_rows, columns), "seq", split_axis=0, concat_axis=0, tiled=True
    )
    return returned.reshape(block_rows, columns)


def routed_local(queries, key_states, value_states, grad_output, partners, global_blocks):
    devices = lax.axis_size("seq")
    block_rows = queries.shape[0]
    features = queries.shape[1]
    key_value = jnp.concatenate([key_states, value_states], axis=1)
    table_rows = []
    table_rows = table_rows + [partners[0], partners[1], partners[2]]
    table_rows = table_rows + [
        jnp.full((devices,), global_blocks[0], jnp.int32),
        jnp.full((devices,), global_blocks[1], jnp.int32),
    ]
    route_table = jnp.stack(table_rows)
    fetched = route_forward(key_value, route_table, devices)
    padded = extended(key_value, (("seq", 0),), block_rows)
    left_block = padded[:block_rows]
    right_block = padded[2 * block_rows :]
    offset = 0
    random_blocks = [fetched[offset], fetched[offset + 1], fetched[offset + 2]]
    global_rows = [fetched[offset + 3], fetched[offset + 4]]
    key_rows = jnp.concatenate(
        [key_value, left_block, right_block] + random_blocks + global_rows, axis=0
    )
    attended, grad_queries, grad_pair = attend(queries, key_rows, grad_output)
    grad_parts = grad_pair.reshape(8, block_rows, 2 * features)
    grad_total = grad_parts[0]
    returning = []
    grad_total = grad_total + from_behind(grad_parts[1], "seq", -1)
    grad_total = grad_total + from_behind(grad_parts[2], "seq", 1)
    returning = returning + [grad_parts[3], grad_parts[4], grad_parts[5]]
    returning = returning + [grad_parts[6], grad_parts[7]]
    grad_total = grad_total + route_back(jnp.stack(returning), route_table, devices)
    return (
        attended,
        grad_queries,
        grad_total[:, :features].astype(jnp.bfloat16),
        grad_total[:, features:].astype(jnp.bfloat16),
    )


ORDER = [
    "p0",
    "c0",
    "p1",
    "e0",
    "c1",
    "f0",
    "s0",
    "p2",
    "e1",
    "c2",
    "s1",
    "p3",
    "e2",
    "c3",
    "f2",
    "s2",
    "f1",
    "e3",
    "f3",
    "s3",
]
LISTED = 8
TO_LOG2 = 1.0 / (math.log(2.0) * math.sqrt(HD))
VMEM_LIMIT = 40 * 1024 * 1024
PAIR_LIMIT = 40 * 1024 * 1024


def matmul(a, b, contract_a, contract_b):
    return lax.dot_general(
        a, b, (((contract_a,), (contract_b,)), ((), ())), preferred_element_type=jnp.float32
    )


def placed(rows, side):
    blank = jnp.zeros_like(rows)
    return jnp.concatenate([rows, blank] if side == 0 else [blank, rows], axis=0)


def listed_times(partners_ref, globals_ref, query_block, key_block, devices):
    count = jnp.int32(0)
    entries = [query_block, lax.rem(query_block + devices - 1, devices)]
    entries += [lax.rem(query_block + 1, devices)]
    entries += [partners_ref[r, query_block] for r in range(partners_ref.shape[0])]
    entries += [globals_ref[g] for g in range(globals_ref.shape[0])]
    for entry in entries:
        count = count + jnp.where(entry == key_block, 1, 0)
    return count


def chosen(index, values):
    result = values[0]
    for at in range(1, len(values)):
        result = jnp.where(index == at, values[at], result)
    return result


def pairs_kernel(plan, partners_ref, globals_ref, *refs):
    pairs, query_moves, key_moves, carried = plan
    queries, keys = len(query_moves), len(key_moves)
    query_refs = refs[: 2 * queries]
    key_refs = refs[2 * queries : 2 * (queries + keys)]
    refs = refs[2 * (queries + keys) :]
    if carried:
        acc_in, run_in = refs[:2]
        refs = refs[2:]
    e_ref, u_ref, acc_ref, run_ref, pair_ref = refs[:5]
    q_now, do_now, k_now, v_now, low_kept, both_kept, peak_kept, v_kept, kt_kept, dt_kept = refs[5:]
    step = pl.program_id(0)
    total_steps = pl.num_programs(0) - 1
    per_pair = total_steps // len(pairs)
    now = jnp.minimum(step, total_steps - 1)
    then = jnp.maximum(step - 1, 0)
    slot, old_slot = lax.rem(step, 2), lax.rem(step + 1, 2)
    pair_now, pair_then = now // per_pair, then // per_pair
    group = lax.rem(then, per_pair)
    for at in range(queries):

        @pl.when(chosen(pair_now, [q for q, _ in pairs]) == at)
        def _():
            q_now[...] = query_refs[2 * at][...]
            do_now[...] = query_refs[2 * at + 1][...]

    for at in range(keys):

        @pl.when(chosen(pair_now, [k for _, k in pairs]) == at)
        def _():
            k_now[...] = key_refs[2 * at][...]
            v_now[...] = key_refs[2 * at + 1][...]

    chunk = q_now.shape[0] // 2
    devices = lax.axis_size("seq")
    me = lax.axis_index("seq")
    count = listed_times(
        partners_ref,
        globals_ref,
        me ^ chosen(pair_then, [query_moves[q] for q, _ in pairs]),
        me ^ chosen(pair_then, [key_moves[k] for _, k in pairs]),
        devices,
    ).astype(jnp.float32)
    bias = jnp.log2(jnp.full((1, chunk), jnp.maximum(count, 1.0), jnp.float32))
    bias = jnp.where(count > 0.0, bias, -1e30)
    member = chosen(pair_then, [q for q, _ in pairs])
    first_head = 2 * group

    key_rows = k_now[...]
    values = v_now[...]
    keys_twice = jnp.concatenate([key_rows, key_rows], axis=1)
    q_t = q_now[...].T.astype(jnp.float32) * TO_LOG2
    q_high = q_t.astype(jnp.bfloat16)
    q_low = (q_t - q_high.astype(jnp.float32)).astype(jnp.bfloat16)
    k_t = key_rows.T
    v_t = values.T
    v_kept[slot] = values
    kt_kept[slot] = k_t
    dt_kept[slot] = do_now[...].T
    ones = jnp.ones((16, key_rows.shape[0]), jnp.bfloat16)
    units = [(side, at) for side in range(2) for at in range(2)]
    halves = [slice(0, HD), slice(HD, 2 * HD)]
    lanes = [slice(at * chunk, (at + 1) * chunk) for at in range(2)]
    scores = {}
    lows = {}
    centred = {}

    def products(n):
        side, at = units[n]
        both_q = [placed(x[halves[side], lanes[at]], side) for x in (q_high, q_low)]
        scores[n] = matmul(keys_twice, jnp.concatenate(both_q, axis=0), 1, 0)

    def exponents(n):
        side, at = units[n]
        peak = jnp.max(scores[n], axis=0, keepdims=True)
        low = jnp.exp2(scores.pop(n) - peak).astype(jnp.bfloat16)
        e_ref[0, side, :, lanes[at]] = low
        low_kept[slot, side, :, lanes[at]] = low
        peak_kept[slot, side : side + 1, lanes[at]] = peak
        lows[n] = low

    def sums(n):
        side, at = units[n]
        left = jnp.concatenate([v_t[halves[side]], k_t[halves[side]], ones], axis=0)
        both_kept[slot, side, :, lanes[at]] = matmul(left, lows.pop(n), 1, 0)

    def centre(n):
        side, at = units[n]
        cols = lanes[at]
        do_t = dt_kept[old_slot, halves[side], cols]
        upper = both_kept[old_slot, side, :HD, cols]
        total = both_kept[old_slot, side, 2 * HD : 2 * HD + 1, cols]
        dots = jnp.sum(upper * do_t.astype(jnp.float32), axis=0, keepdims=True)
        mean = dots / total
        grad = matmul(v_kept[old_slot], placed(do_t, side), 1, 0)
        shifted = low_kept[old_slot, side, :, cols] * (grad - mean).astype(jnp.bfloat16)
        u_ref[0, side, :, cols] = shifted
        centred[n] = (shifted, total, dots, mean)

    def finish(n):
        side, at = units[n]
        cols = lanes[at]
        shifted, total, dots, mean = centred.pop(n)
        both = both_kept[old_slot, side, : 2 * HD, cols]
        moved = matmul(kt_kept[old_slot, halves[side]], shifted, 1, 0) + mean * both[HD:]
        peak = peak_kept[old_slot, side : side + 1, cols] + bias
        head = first_head + side
        row = 3 * side
        old = run_ref[member, group, row : row + 1, cols]
        top = jnp.maximum(old, peak)
        keep = jnp.exp2(old - top)
        take = jnp.exp2(peak - top)
        acc_ref[member, head, : 2 * HD, cols] = (
            acc_ref[member, head, : 2 * HD, cols] * keep + both * take
        )
        acc_ref[member, head, 2 * HD :, cols] = (
            acc_ref[member, head, 2 * HD :, cols] * keep + moved * take
        )
        total = run_ref[member, group, row + 1 : row + 2, cols] * keep + total * take
        dots = run_ref[member, group, row + 2 : row + 3, cols] * keep + dots * take
        for at_row, value in enumerate((top, total, dots)):
            run_ref[member, group, row + at_row : row + at_row + 1, cols] = value
        for at_row, value in enumerate((peak, mean)):
            pair_ref[0, row + at_row : row + at_row + 1, cols] = value

    stages = dict(p=products, e=exponents, s=sums, c=centre, f=finish)
    for name in ORDER:
        stages[name[0]](int(name[1:]))

    @pl.when(step == 0)
    def _():
        acc_ref[...] = jnp.zeros_like(acc_ref)
        run_ref[...] = jnp.zeros_like(run_ref)
        for member_at in range(acc_ref.shape[0]):
            if member_at < carried:
                acc_ref[member_at] = acc_in[member_at]
                run_ref[member_at] = run_in[member_at]
            else:
                for row in (0, 3):
                    shape = (run_ref.shape[1], 1, run_ref.shape[3])
                    run_ref[member_at, :, row : row + 1] = jnp.full(shape, -1e30, jnp.float32)


def head_pairs(features):
    return features // (2 * HD)


def column_spec(rows, offset):
    return pl.BlockSpec((rows, 2 * HD), lambda p: (0, p + offset))


def step_spec(offset, steps, used, last, *block):
    def index(p):
        now = jnp.minimum(p, last)
        live = sum(jnp.where(now // steps == at, 1, 0) for at in used)
        return (0, lax.rem(now, steps) * live + offset)

    return pl.BlockSpec(block, index)


def pair_terms(tables, pairs, query_blocks, key_blocks, running):
    query_moves, query_arrays = zip(*query_blocks)
    key_moves, key_arrays = zip(*key_blocks)
    rows, columns = query_arrays[0].shape
    keys = key_arrays[0].shape[0]
    features = columns // 2
    steps = head_pairs(features)
    heads = 2 * steps
    total = len(pairs) * steps
    members = len(query_arrays)
    state = [] if running is None else list(running)
    carried = state[0].shape[0] if state else 0
    plan = (pairs, query_moves, key_moves, carried)
    acc = jax.ShapeDtypeStruct((members, heads, 3 * HD, rows), jnp.float32)
    run = jax.ShapeDtypeStruct((members, steps, 8, rows), jnp.float32)
    stat = jax.ShapeDtypeStruct((total, 8, rows), jnp.float32)
    big = jax.ShapeDtypeStruct((total, 2, keys, rows), jnp.bfloat16)
    operands = []
    in_specs = [pl.BlockSpec(memory_space=pltpu.SMEM)] * 2
    for kind, arrays in ((0, query_arrays), (1, key_arrays)):
        for which, array in enumerate(arrays):
            used = [at for at, pair in enumerate(pairs) if pair[kind] == which]
            length = array.shape[0]
            in_specs.append(step_spec(0, steps, used, total - 1, length, 2 * HD))
            in_specs.append(step_spec(steps, steps, used, total - 1, length, 2 * HD))
            operands += [array, array]
    whole = pl.BlockSpec(memory_space=pltpu.VMEM)
    in_specs += [whole] * len(state)
    now = lambda p: (jnp.minimum(p, total - 1), 0, 0, 0)
    then = lambda p: (jnp.maximum(p - 1, 0), 0, 0, 0)
    block = (1, 2, keys, rows)
    tile = pltpu.VMEM((rows, 2 * HD), jnp.bfloat16)
    return pl.pallas_call(
        lambda *refs: pairs_kernel(plan, *refs),
        grid=(total + 1,),
        in_specs=in_specs,
        out_specs=[
            pl.BlockSpec(block, now),
            pl.BlockSpec(block, then),
            whole,
            whole,
            pl.BlockSpec((1, 8, rows), lambda p: then(p)[:3]),
        ],
        out_shape=[big, big, acc, run, stat],
        scratch_shapes=[
            tile,
            tile,
            pltpu.VMEM((keys, 2 * HD), jnp.bfloat16),
            pltpu.VMEM((keys, 2 * HD), jnp.bfloat16),
            pltpu.VMEM((2, 2, keys, rows), jnp.bfloat16),
            pltpu.VMEM((2, 2, 2 * HD + 16, rows), jnp.float32),
            pltpu.VMEM((2, 8, rows), jnp.float32),
            pltpu.VMEM((2, keys, 2 * HD), jnp.bfloat16),
            pltpu.VMEM((2, 2 * HD, keys), jnp.bfloat16),
            pltpu.VMEM((2, 2 * HD, rows), jnp.bfloat16),
        ],
        compiler_params=pltpu.CompilerParams(vmem_limit_bytes=PAIR_LIMIT),
        cost_estimate=pl.CostEstimate(
            flops=len(pairs) * 8 * heads * HD * rows * keys,
            transcendentals=len(pairs) * heads * rows * keys,
            bytes_accessed=len(pairs) * 4 * heads * rows * keys,
        ),
    )(*tables, *operands, *state)


def joined(mine, other, side):
    at = 3 * side
    top = jnp.maximum(mine[at : at + 1], other[at : at + 1])
    here = jnp.exp2(mine[at : at + 1] - top)
    there = jnp.exp2(other[at : at + 1] - top)
    inverse = 1.0 / (mine[at + 1 : at + 2] * here + other[at + 1 : at + 2] * there)
    mean = (mine[at + 2 : at + 3] * here + other[at + 2 : at + 3] * there) * inverse
    share = other[at + 1 : at + 2] * there * inverse
    return top, inverse, mean, share


def key_kernel(*refs):
    out = refs[-1]
    features = out.shape[1] // 2
    scale = 1.0 / math.sqrt(HD)
    k_total = None
    v_total = None
    for at in range(0, len(refs) - 1, 7):
        e_ref, u_ref, q_ref, do_ref, pair_ref, mine, other = refs[at : at + 7]
        q_t = q_ref[...].T.astype(jnp.float32)
        do_t = do_ref[...].T.astype(jnp.float32)
        for side in range(2):
            rows = slice(side * HD, (side + 1) * HD)
            top, inverse, mean, _ = joined(mine.at[0, 0], other.at[0, 0], side)
            factor = jnp.exp2(pair_ref[0, 3 * side : 3 * side + 1] - top) * inverse
            shift = pair_ref[0, 3 * side + 1 : 3 * side + 2] - mean
            scaled_q = q_t[rows] * (factor * scale)
            for_e = jnp.concatenate(
                [
                    placed((scaled_q * shift).astype(jnp.bfloat16), side),
                    placed((do_t[rows] * factor).astype(jnp.bfloat16), side),
                ],
                axis=0,
            )
            from_e = matmul(e_ref[0, side], for_e, 1, 1)
            from_u = matmul(u_ref[0, side], placed(scaled_q.astype(jnp.bfloat16), side), 1, 1)
            k_part = from_e[:, : 2 * HD] + from_u
            v_part = from_e[:, 2 * HD :]
            k_total = k_part if k_total is None else k_total + k_part
            v_total = v_part if v_total is None else v_total + v_part
    at = pl.program_id(0) * (2 * HD)
    out[:, pl.ds(pl.multiple_of(at, 2 * HD), 2 * HD)] = k_total.astype(out.dtype)
    at = at + features
    out[:, pl.ds(pl.multiple_of(at, 2 * HD), 2 * HD)] = v_total.astype(out.dtype)


def member_rows(member, rows):
    return pl.BlockSpec((1, 1, 8, rows), lambda p: (member, p, 0, 0))


def key_terms(entries, mine, theirs, dtype):
    operands = []
    in_specs = []
    for member, (e, u, query_grad, stat, base) in enumerate(entries):
        _, _, keys, rows = e.shape
        steps = head_pairs(query_grad.shape[1] // 2)
        block = pl.BlockSpec((1, 2, keys, rows), lambda p, base=base: (p + base, 0, 0, 0))
        operands += [e, u, query_grad, query_grad, stat, mine, theirs]
        in_specs += [
            block,
            block,
            column_spec(rows, 0),
            column_spec(rows, steps),
            pl.BlockSpec((1, 8, rows), lambda p, base=base: (p + base, 0, 0)),
            member_rows(member, rows),
            member_rows(1 - member, rows),
        ]
    heads = 2 * steps
    return pl.pallas_call(
        key_kernel,
        grid=(steps,),
        in_specs=in_specs,
        out_specs=pl.BlockSpec(memory_space=pltpu.VMEM),
        out_shape=jax.ShapeDtypeStruct((keys, 2 * heads * HD), dtype),
        name="key_terms",
        compiler_params=pltpu.CompilerParams(vmem_limit_bytes=VMEM_LIMIT),
        cost_estimate=pl.CostEstimate(
            flops=len(entries) * 6 * heads * HD * rows * keys,
            transcendentals=0,
            bytes_accessed=len(entries) * 4 * heads * rows * keys,
        ),
    )(*operands)


def attend_kernel(acc, mine, out):
    for side in range(2):
        inverse = 1.0 / mine[0, 0, 3 * side + 1 : 3 * side + 2]
        out[side * HD : (side + 1) * HD] = (acc[0, side] * inverse).astype(out.dtype)


def acc_rows(member, which, rows):
    return pl.BlockSpec((1, 2, HD, rows), lambda p: (member, p, which, 0))


def attend_terms(member, acc, mine):
    _, heads, _, rows = acc.shape
    return pl.pallas_call(
        attend_kernel,
        grid=(heads // 2,),
        in_specs=[acc_rows(member, 0, rows), member_rows(member, rows)],
        out_specs=pl.BlockSpec((2 * HD, rows), lambda p: (p, 0)),
        out_shape=jax.ShapeDtypeStruct((heads * HD, rows), jnp.bfloat16),
        name="attend_terms",
        compiler_params=pltpu.CompilerParams(vmem_limit_bytes=VMEM_LIMIT),
        cost_estimate=pl.CostEstimate(
            flops=heads * HD * rows, transcendentals=0, bytes_accessed=6 * heads * HD * rows
        ),
    )(acc, mine)


def query_kernel(own, *refs):
    if own:
        first, second, mine, other, upper, came, out_o, out_q = refs
    else:
        first, second, mine, other, out_q = refs
    scale = 1.0 / math.sqrt(HD)
    outs = []
    grads = []
    for side in range(2):
        top, inverse, mean, share = joined(mine.at[0, 0], other.at[0, 0], side)
        factor = jnp.exp2(mine[0, 0, 3 * side : 3 * side + 1] - top) * inverse
        grads.append((second[0, side] - first[0, side] * mean) * (factor * scale))
        if own:
            theirs = came[side * HD : (side + 1) * HD].astype(jnp.float32) * share
            outs.append(upper[0, side] * factor + theirs)
    out_q[...] = jnp.concatenate(grads, axis=0).T.astype(out_q.dtype)
    if own:
        out_o[...] = jnp.concatenate(outs, axis=0).T.astype(out_o.dtype)


def query_terms(member, acc, mine, theirs, came):
    _, heads, _, rows = acc.shape
    own = came is not None
    in_specs = [acc_rows(member, 1, rows), acc_rows(member, 2, rows)]
    in_specs += [member_rows(member, rows), member_rows(1 - member, rows)]
    operands = [acc, acc, mine, theirs]
    shapes = [jax.ShapeDtypeStruct((rows, heads * HD), jnp.float32 if own else jnp.bfloat16)]
    if own:
        in_specs += [acc_rows(member, 0, rows), pl.BlockSpec((2 * HD, rows), lambda p: (p, 0))]
        operands += [acc, came]
        shapes = [jax.ShapeDtypeStruct((rows, heads * HD), jnp.bfloat16)] + shapes
    return pl.pallas_call(
        lambda *refs: query_kernel(own, *refs),
        grid=(heads // 2,),
        in_specs=in_specs,
        out_specs=[column_spec(rows, 0)] * len(shapes),
        out_shape=shapes,
        name="query_own" if own else "query_send",
        compiler_params=pltpu.CompilerParams(vmem_limit_bytes=VMEM_LIMIT),
        cost_estimate=pl.CostEstimate(
            flops=8 * heads * HD * rows, transcendentals=0, bytes_accessed=16 * heads * HD * rows
        ),
    )(*operands)


def summed(parts):
    total = parts[0][...].astype(jnp.float32)
    for part in parts[1:]:
        total = total + part[...].astype(jnp.float32)
    return total


def final_kernel(splits, *refs):
    total = summed(refs[:-splits])
    for at, out in enumerate(refs[-splits:]):
        columns = out.shape[1]
        out[...] = total[:, at * columns : (at + 1) * columns].astype(jnp.bfloat16)


def final_sums(parts, splits):
    rows, columns = parts[0].shape
    return pl.pallas_call(
        lambda *refs: final_kernel(splits, *refs),
        in_specs=[pl.BlockSpec(memory_space=pltpu.VMEM)] * len(parts),
        out_specs=[pl.BlockSpec(memory_space=pltpu.VMEM)] * splits,
        out_shape=[jax.ShapeDtypeStruct((rows, columns // splits), jnp.bfloat16)] * splits,
        name="final_sums",
    )(*parts)


def swapped(x, offset):
    devices = lax.axis_size("seq")
    return lax.ppermute(x, "seq", [(i, i ^ offset) for i in range(devices)])


def pack_kernel(k_ref, v_ref, q_ref, do_ref, kv_ref, qd_ref):
    features = k_ref.shape[1]
    qd_ref[:, :features] = q_ref[...]
    qd_ref[:, features:] = do_ref[...]
    kv_ref[:, :features] = k_ref[...]
    kv_ref[:, features:] = v_ref[...]


def packed(key_states, value_states, queries, grad_output):
    rows, features = queries.shape
    both = jax.ShapeDtypeStruct((rows, 2 * features), queries.dtype)
    whole = pl.BlockSpec(memory_space=pltpu.VMEM)
    return pl.pallas_call(
        pack_kernel,
        in_specs=[whole] * 4,
        out_specs=[whole] * 2,
        out_shape=[both, both],
        name="pack",
    )(key_states, value_states, queries, grad_output)


def after(x, earlier):
    return lax.optimization_barrier((x, earlier))[0]


def dense_local(queries, key_states, value_states, grad_output, partners, global_blocks):
    devices = lax.axis_size("seq")
    far = devices // 2
    tables = (partners, global_blocks)
    key_value, query_grad = packed(key_states, value_states, queries, grad_output)
    offsets = list(range(far))
    neighbours = [o for o in offsets if o and o & (o - 1) == 0]
    relayed = [o for o in offsets if o and o not in neighbours]
    query_blocks = [(0, query_grad), (far, swapped(query_grad, far))]
    blocks = {0: key_value}
    for o in neighbours:
        blocks[o] = swapped(key_value, o)
    saved = {}
    last = [None]

    def run(pairs, members, running):
        used = sorted({k for _, k in pairs})
        key_blocks = [(k, blocks[k]) for k in used]
        if last[0] is not None:
            key_blocks = [(k, after(x, last[0])) for k, x in key_blocks]
        plan = tuple((q, used.index(k)) for q, k in pairs)
        e, u, acc, state, stat = pair_terms(
            tables, plan, query_blocks[:members], key_blocks, running
        )
        for at, (q, k) in enumerate(pairs):
            base = at * (stat.shape[0] // len(pairs))
            saved[(q, k)] = (e, u, query_blocks[q][1], stat, base)
        last[0] = stat
        return (acc, state)

    running = run([(0, 0)], 1, None)
    for o in neighbours[:-1]:
        running = run([(0, o)], 1, running)
    for o in relayed:
        lowest = o & -o
        blocks[o] = swapped(after(blocks[o - lowest], last[0]), lowest)
    rest = [(0, neighbours[-1])] + [(1, o) for o in [0] + neighbours]
    running = run(rest, 2, running)
    acc, mine = run([(q, o) for o in relayed for q in (1, 0)], 2, running)
    theirs = swapped(mine, far)
    upper = attend_terms(1, acc, mine)
    came_upper = swapped(after(upper, theirs), far)
    key_parts = []
    for k in offsets[:0:-1]:
        entries = [saved[(q, k)] for q in range(2)]
        terms = key_terms(entries, mine, after(theirs, last[0]), jnp.bfloat16)
        key_parts.append(swapped(terms, k))
        last[0] = terms
        if len(key_parts) == 1:
            sent = query_terms(1, acc, mine, after(theirs, terms), None)[0]
            came = swapped(sent, far)
            last[0] = sent
    own_entries = [saved[(q, 0)] for q in range(2)]
    own_keys = key_terms(own_entries, mine, after(theirs, last[0]), jnp.float32)
    came_upper = after(came_upper, own_keys)
    attended, own_queries = query_terms(0, acc, mine, theirs, came_upper)
    came = after(came, own_queries)
    grad_queries = final_sums([own_queries, came], 1)[0]
    key_parts = [after(x, grad_queries) for x in key_parts]
    grad_keys, grad_values = final_sums([own_keys] + key_parts, 2)
    return (attended, grad_queries, grad_keys, grad_values)


def paired(devices):
    return 4 <= devices <= LISTED and devices & (devices - 1) == 0


def local(*operands):
    if paired(lax.axis_size("seq")):
        return dense_local(*operands)
    return routed_local(*operands)


def solution(mesh):
    in_specs = (
        P(("batch", "seq"), None),
        P(("batch", "seq"), None),
        P(("batch", "seq"), None),
        P(("batch", "seq"), None),
        P("batch", None),
        P("batch"),
    )
    out_specs = (
        P(("batch", "seq"), None),
        P(("batch", "seq"), None),
        P(("batch", "seq"), None),
        P(("batch", "seq"), None),
    )
    step = jax.shard_map(
        local, mesh=mesh, in_specs=in_specs, out_specs=out_specs, check_vma=False
    )
    devices = mesh.shape["seq"]
    if paired(devices):
        return step
    return step
```
